32 devices in a mesh: grp: 2 (over y), ctx: 8 (over z, x), head: 2 (over core).
Axes of the slice: x: 2, y: 2, z: 4, core: 2. Of those that a mesh axis runs over, the one named last changes fastest.
Arguments:
- queries: bfloat16 [4, 64, 128], P('grp', 'head'), parts along dimension 0, may hold values from -8 to 8
- keys: bfloat16 [8192, 8, 128], P(('grp', 'ctx'), 'head'), parts along dimension 0, may hold values from -8 to 8
- values: bfloat16 [8192, 8, 128], P(('grp', 'ctx'), 'head'), parts along dimension 0, may hold values from -6 to 6
- new_keys: bfloat16 [4, 8, 128], P('grp', 'head'), parts along dimension 0, may hold values from -6 to 6
- new_values: bfloat16 [4, 8, 128], P('grp', 'head'), parts along dimension 0, may hold values from -6 to 6
- keep: int32 [128, 8], P('grp'), parts along dimension 0, may hold values 0 or 1
- block_source: int32 [16], P('grp'), parts along dimension 0, may hold values from 0 to 7, each once
- out_weight: bfloat16 [8192, 8192], P('head', 'ctx'), may hold values from -0.0625 to 0.0625
- readout: bfloat16 [4, 8192], P('grp', ('ctx', 'head')), parts along dimension 0, may hold values from -0.0625 to 0.0625
- gain: float32 [8192], P(('ctx', 'head')), may hold values from 0.5 to 1.5
Outputs:
- projected: bfloat16 [128, 2, 8192], P('grp', None, ('ctx', 'head')), parts along dimension 0
- logits: float32 [128, 2], P('grp'), parts along dimension 0
- attribution: float32 [16], P('grp'), parts along dimension 0
The draws below stay inside these ranges and needn't reach their ends.
There are 2 independent parts, one for each index of `grp`. The reference program is written for one: setup_inputs(seed, part) draws one part's arguments, and reference() takes and returns one part's arrays. A program takes and returns all parts, laid end to end along the dimension named above; an argument that names none is the same for every part. Nothing has to cross between parts.
Inputs may be any that keep to these rules, and one draw needn't show every extreme that they name: `block_source`: each source appears exactly once.
All inputs are finite; a program needn't handle non-finite values.
Results may differ from the reference program's by a relative error of at most 0.008.
Values may be sent and summed in bfloat16 or wider, within the bound.
A program may use at most 128 MiB of HBM per device.

```python
import jax
import jax.numpy as jnp
from jax import lax

D_MODEL = 8192
Q_HEADS = 64
KV_HEADS = 8
HEAD_DIM = 128
ABL = 64
RESP = 2
BLOCK = 512
SOURCES = 8
CONTEXT = 4096


def draw_keys(key, part):
    base = jax.random.normal(jax.random.fold_in(key, 1), (CONTEXT, KV_HEADS, HEAD_DIM), jnp.float32)
    return base.astype(jnp.bfloat16)


def draw_queries(key, part):
    base = jax.random.normal(jax.random.fold_in(key, 2), (RESP, Q_HEADS, HEAD_DIM), jnp.float32)
    return base.astype(jnp.bfloat16)


def touch_ends(result, own_key, least, top_value):
    dims = result.shape
    index_at = [jax.random.randint(jax.random.fold_in(own_key, axis), (), 0, dims[axis]) for axis in range(len(dims))]
    result = result.at[tuple(index_at)].set(least)
    longest = dims.index(max(dims))
    index_at[longest] = (index_at[longest] + 1) % dims[longest]
    return result.at[tuple(index_at)].set(top_value)


def block_scale(stream_key, shape, shards, least, top_value):
    level = 1.0
    for position, blocks in shards:
        draws = jax.random.uniform(jax.random.fold_in(jax.random.fold_in(stream_key, 6), position), (blocks,), jnp.float32, least / len(shards), top_value / len(shards))
        level = level * jnp.repeat(jnp.exp(draws), shape[position] // blocks).reshape((-1,) + (1,) * (len(shape) - 1 - position))
    return level


def scatter_about(key, extent, width, reach, split=(), held_as=jnp.bfloat16):
    level = block_scale(key, extent, split, -0.22, 0.18) if split else 1.0
    values = jax.random.normal(key, extent, jnp.float32) * width * level
    return jnp.minimum(jnp.maximum(values, -reach), reach).astype(held_as)


def setup_inputs(seed: int = 0, part: int = 0) -> dict:
    seeds = jax.random.split(jax.random.key(seed), 11)
    part_keys = jax.random.split(jax.random.fold_in(seeds[10], part), 11)
    return {
        "queries": draw_queries(jax.random.fold_in(jax.random.fold_in(seeds[10], part), 71), part),
        "keys": draw_keys(jax.random.fold_in(jax.random.fold_in(seeds[10], part), 71), part),
        "values": scatter_about(part_keys[2], (CONTEXT, KV_HEADS, HEAD_DIM), 1.0, 6.0, ((0, 8), (1, 2))),
        "new_keys": scatter_about(part_keys[3], (RESP, KV_HEADS, HEAD_DIM), 1.0, 6.0, ((1, 2),)),
        "new_values": scatter_about(part_keys[4], (RESP, KV_HEADS, HEAD_DIM), 1.0, 6.0, ((1, 2),)),
        "keep": touch_ends((jax.random.randint(part_keys[5], (ABL, SOURCES), 0, 2) < 1).astype(jnp.int32), jax.random.fold_in(part_keys[5], 1), 0, 1),
        "block_source": jax.random.permutation(part_keys[6], SOURCES).astype(jnp.int32),
        "out_weight": scatter_about(seeds[7], (Q_HEADS * HEAD_DIM, D_MODEL), (Q_HEADS * HEAD_DIM) ** -0.5, 0.0625, ((0, 2), (1, 8))),
        "readout": scatter_about(part_keys[8], (RESP, D_MODEL), D_MODEL ** -0.5, 0.0625, ((1, 16),)),
        "gain": jnp.clip(1.0 + 0.1 * jax.random.normal(seeds[9], (D_MODEL,), jnp.float32), 0.5, 1.5),
    }


EPSILON = 1e-05
RIDGE = 1.0

def surrogate(keep, logits):
    design = keep.astype(jnp.float32)
    targets = lax.optimization_barrier(jnp.sum(logits, axis=1))
    centered = design - lax.optimization_barrier(jnp.mean(design, axis=0))[None, :]
    target_dev = targets - jnp.mean(targets)
    gram_matrix = jnp.dot(centered.T, centered, precision=lax.Precision.HIGHEST) + RIDGE * jnp.eye(design.shape[1], dtype=jnp.float32)
    right_hand = jnp.dot(centered.T, target_dev, precision=lax.Precision.HIGHEST)
    factor = jnp.linalg.cholesky(gram_matrix)
    lower_sol = jax.scipy.linalg.solve_triangular(factor, right_hand, lower=True)
    return jax.scipy.linalg.solve_triangular(factor.T, lower_sol, lower=False)

def reference(queries, keys, values, new_keys, new_values, keep, block_source, out_weight, readout, gain):
    group = Q_HEADS // KV_HEADS
    rows_per = RESP * group
    scale = HEAD_DIM ** (-0.5)
    grouped = queries.reshape(RESP, KV_HEADS, group, HEAD_DIM).transpose(1, 0, 2, 3).reshape(KV_HEADS, rows_per, HEAD_DIM)
    key_heads = keys.transpose(1, 0, 2)
    value_heads = values.reshape(SOURCES, BLOCK, KV_HEADS, HEAD_DIM).transpose(2, 0, 1, 3)

    def one_head(operands):
        query_rows, key_rows, value_rows = operands
        scores = jnp.dot(query_rows.astype(jnp.float32), key_rows.T.astype(jnp.float32), preferred_element_type=jnp.float32) * scale
        scores = scores.reshape(rows_per, SOURCES, BLOCK)
        block_top = lax.optimization_barrier(jnp.max(scores, axis=-1))
        expo = jnp.exp(scores - block_top[..., None])
        block_total = lax.optimization_barrier(jnp.sum(expo, axis=-1))
        block_sum = jnp.einsum('rsj,sjd->rsd', expo.astype(jnp.bfloat16).astype(jnp.float32), value_rows.astype(jnp.float32))
        return (block_top, block_total, block_sum)
    block_top, block_total, block_sum = lax.map(one_head, (grouped, key_heads, value_heads))
    pair_count = KV_HEADS * rows_per
    block_top = block_top.reshape(pair_count, SOURCES)
    block_total = block_total.reshape(pair_count, SOURCES)
    block_sum = block_sum.reshape(pair_count, SOURCES, HEAD_DIM)
    own_scores = jnp.einsum('hrd,ihd->hri', grouped.astype(jnp.float32), new_keys.astype(jnp.float32)) * scale
    step_row = jnp.arange(rows_per, dtype=jnp.int32) // group
    allowed = jnp.arange(RESP, dtype=jnp.int32)[None, :] <= step_row[:, None]
    own_scores = jnp.where(allowed[None], own_scores, -jnp.inf)
    own_top = lax.optimization_barrier(jnp.max(own_scores, axis=-1))
    own_expo = jnp.where(allowed[None], jnp.exp(own_scores - own_top[..., None]), 0.0)
    own_total = lax.optimization_barrier(jnp.sum(own_expo, axis=-1)).reshape(pair_count)
    own_sum = jnp.einsum('hri,ihd->hrd', own_expo.astype(jnp.bfloat16).astype(jnp.float32), new_values.astype(jnp.float32)).reshape(pair_count, HEAD_DIM)
    own_top = own_top.reshape(pair_count)
    kept = keep[:, block_source] > 0
    overall = lax.optimization_barrier(jnp.max(jnp.where(kept[:, None, :], block_top[None], -jnp.inf), axis=-1))
    overall = jnp.maximum(overall, own_top[None])
    weights = jnp.where(kept[:, None, :], jnp.exp(block_top[None] - overall[..., None]), 0.0)
    own_weight = jnp.exp(own_top[None] - overall)
    numer = jnp.einsum('apb,pbd->apd', weights, block_sum, precision=lax.Precision.HIGHEST) + own_weight[..., None] * own_sum[None]
    denom = jnp.einsum('apb,pb->ap', weights, block_total, precision=lax.Precision.HIGHEST) + own_weight * own_total[None]
    attended = (numer / denom[..., None]).astype(jnp.bfloat16)
    flat = attended.reshape(ABL, KV_HEADS, RESP, group, HEAD_DIM).transpose(0, 2, 1, 3, 4).reshape(ABL * RESP, Q_HEADS * HEAD_DIM)
    projected = jnp.dot(flat.astype(jnp.float32), out_weight.astype(jnp.float32), preferred_element_type=jnp.float32).astype(jnp.bfloat16).reshape(ABL, RESP, D_MODEL)
    feature = projected.astype(jnp.float32)
    squares = lax.optimization_barrier(jnp.mean(feature * feature, axis=-1))
    dotted = lax.optimization_barrier(jnp.sum(feature * (readout.astype(jnp.float32) * gain[None, :])[None], axis=-1))
    logits = dotted * lax.rsqrt(squares + EPSILON)
    return (projected, logits, surrogate(keep, logits))
```

```python
import functools

import jax
import jax.numpy as jnp
from jax import lax
from jax.experimental import pallas as pl
from jax.experimental.pallas import tpu as pltpu
from jax.sharding import PartitionSpec as P

BLOCK = 512
EPSILON = 1e-05
RIDGE = 1.0
LOW = -1e30
LANES = 128
F32 = jnp.float32
BF16 = jnp.bfloat16
NT = (((1,), (1,)), ((), ()))


def iota(shape, axis):
    return lax.broadcasted_iota(jnp.int32, shape, axis)


def powers(size):
    return [1 << i for i in range(size.bit_length() - 1)]


def slot_count(ctx_size, pairs):
    per = LANES // pairs
    return -(-(ctx_size + 1) // per) * per


def to_row(column):
    return jnp.transpose(jnp.broadcast_to(column, (LANES, LANES)))[0:1, :]


def kernel(
    ctx_size,
    head_size,
    answer_len,
    kv_here,
    features,
    bs_hbm,
    q_hbm,
    k_hbm,
    v_hbm,
    nk_hbm,
    nv_hbm,
    keep_hbm,
    w_hbm,
    readout_hbm,
    gain_hbm,
    proj_ref,
    logit_ref,
    attr_ref,
    bs_ref,
    q_ref,
    k_ref,
    v_ref,
    nk_ref,
    nv_ref,
    keep_ref,
    w_ref,
    readout_ref,
    gain_ref,
    mean_all,
    lse_all,
    flat_ref,
    y_ref,
    order_ref,
    left_ref,
    half_ref,
    far_half,
    stat_all,
    local_sem,
    w_sem,
    mean_sem,
    lse_sem,
    half_sem,
    stat_sem,
):
    grp = lax.axis_index("grp")
    mine = lax.axis_index("ctx")
    core = lax.axis_index("head")
    pairs, width = q_ref.shape
    heads = pairs // answer_len
    group = heads // kv_here
    tokens = k_ref.shape[0]
    sources, ablations = keep_ref.shape
    slots = slot_count(ctx_size, pairs)
    lines = flat_ref.shape[0] // pairs * answer_len
    compact = len(left_ref.shape) == 3
    sides, _, wide = w_ref.shape
    half = wide * sides // head_size
    chunk = half_ref.shape[3]
    partner = lax.rem(core + 1, head_size)
    turn = [partner, core]
    theirs, ours = (0, 1) if compact else (partner, core)
    scale = width ** (-0.5)
    rows = ablations * answer_len
    per = LANES // pairs
    devices = ctx_size * head_size

    loads = [
        pltpu.make_async_copy(source, target, local_sem.at[min(i, 3)])
        for i, (source, target) in enumerate(
            (
                (q_hbm, q_ref),
                (k_hbm, k_ref),
                (v_hbm, v_ref),
                (nk_hbm, nk_ref),
                (nv_hbm, nv_ref),
                (keep_hbm, keep_ref),
                (bs_hbm, bs_ref),
                (readout_hbm, readout_ref),
                (gain_hbm, gain_ref),
            )
        )
    ]
    for copy in loads:
        copy.start()
    copies_w = [
        pltpu.make_async_copy(
            w_hbm.at[:, pl.ds(pl.multiple_of(turn[j] * half, LANES), half)] if compact else w_hbm,
            w_ref.at[j],
            w_sem.at[j],
        )
        for j in range(sides)
    ]
    for copy in copies_w:
        copy.start()

    def flips(position, size):
        return [bit * (1 - 2 * lax.rem(position // bit, 2)) for bit in powers(size)]

    ctx_flips, core_flips = flips(mine, ctx_size), flips(core, head_size)

    def flipped(position, deltas, mask):
        for i, delta in enumerate(deltas):
            if mask >> i & 1:
                position = position + delta
        return position

    def other(mask):
        return (
            grp,
            flipped(mine, ctx_flips, mask // head_size),
            flipped(core, core_flips, mask % head_size),
        )

    barrier = pltpu.get_barrier_semaphore()
    for mask in range(devices - 1, 0, -1):
        pl.semaphore_signal(
            barrier, inc=1, device_id=other(mask), device_id_type=pl.DeviceIdType.MESH
        )

    loads[0].wait()
    loads[1].wait()
    queries = q_ref[...]
    scores = lax.dot_general(queries, k_ref[...], NT, preferred_element_type=F32) * scale
    near = lax.rem(iota((pairs, tokens), 1), kv_here) == lax.rem(
        iota((pairs, tokens), 0) // group, kv_here
    )
    top = jnp.max(jnp.where(near, scores, LOW), axis=1, keepdims=True)
    expo = jnp.where(near, jnp.exp(scores - top), 0.0)
    total = jnp.sum(expo, axis=1, keepdims=True)
    loads[2].wait()
    summed = jnp.dot(expo.astype(BF16), v_ref[...], preferred_element_type=F32)
    mean = summed / total
    lse = top + jnp.log(total)
    lse_all[mine] = to_row(jnp.concatenate([lse] * per, axis=0))
    pieces = mean_all.shape[0]
    some = heads // pieces
    for piece in range(pieces):
        for t in range(answer_len):
            first = t * heads + piece * some
            mean_all[piece, mine, pl.ds(t * some, some), :] = mean[first : first + some].astype(
                BF16
            )

    pl.semaphore_wait(barrier, devices - 1)

    def to_peer(source, send, recv, k):
        place = ctx_size - 1 - k
        return pltpu.make_async_remote_copy(
            src_ref=source,
            dst_ref=source,
            send_sem=send,
            recv_sem=recv,
            device_id=(grp, jnp.where(place <= mine, place - 1, place), core),
            device_id_type=pl.DeviceIdType.MESH,
        )

    def bytes_of(block, send, recv):
        return pltpu.make_async_remote_copy(
            src_ref=block,
            dst_ref=block,
            send_sem=send,
            recv_sem=recv,
            device_id=(grp, mine, partner),
            device_id_type=pl.DeviceIdType.MESH,
        )

    all_lse = bytes_of(lse_all.at[pl.ds(0, ctx_size - 1)], lse_sem.at[0], lse_sem.at[1])
    all_mean = [
        bytes_of(mean_all.at[piece, pl.ds(0, ctx_size - 1)], mean_sem.at[0, piece], mean_sem.at[1, piece])
        for piece in range(pieces)
    ]
    def send_to(peers, kinds):
        for kind in kinds:
            for k in peers:
                if kind < 0:
                    copy = to_peer(lse_all.at[mine], lse_sem.at[0], lse_sem.at[1], k)
                else:
                    copy = to_peer(
                        mean_all.at[kind, mine], mean_sem.at[0, kind], mean_sem.at[1, kind], k
                    )
                copy.start()

    first = range(1)
    later = range(1, ctx_size - 1)
    send_to(first, range(-1, pieces))
    send_to(later, range(-1, pieces))

    for copy in loads[3:]:
        copy.wait()
    owns = nk_ref.shape[0]
    own_scores = lax.dot_general(queries, nk_ref[...], NT, preferred_element_type=F32) * scale
    place = iota((pairs, owns), 1)
    pair = iota((pairs, owns), 0)
    allowed = (lax.rem(place, kv_here) == lax.rem(pair // group, kv_here)) & (
        place // kv_here <= pair // heads
    )
    own_top = jnp.max(jnp.where(allowed, own_scores, LOW), axis=1, keepdims=True)
    own_expo = jnp.where(allowed, jnp.exp(own_scores - own_top), 0.0)
    own_total = jnp.sum(own_expo, axis=1, keepdims=True)
    own_probs = own_expo.astype(BF16).astype(F32)
    own_values = nv_ref[...].astype(F32)
    own_sum = jnp.zeros((pairs, width), F32)
    for i in range(owns):
        own_sum += own_probs[:, i : i + 1] * own_values[i : i + 1, :]
    flat_ref[pl.ds(ctx_size * pairs, pairs), :] = own_sum / own_total
    for slot in range(ctx_size + 1, flat_ref.shape[0] // pairs):
        flat_ref[pl.ds(slot * pairs, pairs), :] = jnp.zeros((pairs, width), F32)
    own_lse = to_row(jnp.concatenate([own_top + jnp.log(own_total)] * per, axis=0))

    keep = keep_ref[...].astype(F32)
    repeat = (iota((rows, ablations), 0) // answer_len == iota((rows, ablations), 1)).astype(F32)
    keep_rows = lax.dot_general(repeat, keep, NT, preferred_element_type=F32)
    lane = iota((1, LANES), 1)
    part = lane // pairs
    same = lax.rem(iota((rows, LANES), 1), pairs) // heads == lax.rem(
        iota((rows, LANES), 0), answer_len
    )
    masks = []
    for tile in range(slots // per):
        source = jnp.full((1, LANES), -1, jnp.int32)
        own_lane = jnp.zeros((1, LANES), F32)
        for k in range(per):
            slot = tile * per + k
            if slot < ctx_size:
                source = jnp.where(part == k, bs_ref[slot], source)
            if slot == ctx_size:
                own_lane = jnp.where(part == k, 1.0, own_lane)
        chosen = (iota((sources, LANES), 0) == source).astype(F32)
        kept = jnp.dot(keep_rows, chosen, preferred_element_type=F32) + own_lane
        masks.append((kept > 0.5) & same)

    eye = (iota((sources, sources), 0) == iota((sources, sources), 1)).astype(F32)
    keep_cols = lax.dot_general(keep, repeat, NT, preferred_element_type=F32)
    gram = lax.dot_general(keep, keep, NT, preferred_element_type=F32)
    count = jnp.sum(keep, axis=1, keepdims=True)
    count_row = jnp.sum(keep_rows, axis=0, keepdims=True) / answer_len
    system = gram - count * count_row / ablations + RIDGE * eye
    centered = keep_cols - count / ablations

    def sweep(k, state):
        on_row = iota((sources, sources), 0) == k
        on_col = iota((sources, sources), 1) == k
        row = jnp.sum(jnp.where(on_row, state, 0.0), axis=0, keepdims=True)
        col = jnp.sum(jnp.where(on_col, state, 0.0), axis=1, keepdims=True)
        pivot = jnp.sum(jnp.where(on_col[0:1], row, 0.0), axis=1, keepdims=True)
        inverse = 1.0 / pivot
        return jnp.where(
            on_row,
            jnp.where(on_col, -inverse, row * inverse),
            jnp.where(on_col, col * inverse, state - col * (row * inverse)),
        )

    swept = lax.fori_loop(0, sources, sweep, system, unroll=sources <= 8)
    solver = -jnp.dot(swept, centered, precision=lax.Precision.HIGHEST, preferred_element_type=F32)

    if compact:
        spot = iota((1, heads * lines), 1)
        line = lax.rem(spot, lines)
        wanted = (
            line // answer_len * pairs + lax.rem(line, answer_len) * heads + spot // lines
        )
        order_ref[...] = (iota(order_ref.shape, 0) == wanted).astype(BF16)
    all_lse.wait_recv()

    def make_coef():
        tops = []
        for tile in range(slots // per):
            line = jnp.full((1, LANES), LOW, F32)
            for k in range(per):
                slot = tile * per + k
                if slot <= ctx_size:
                    here = lse_all[slot] if slot < ctx_size else own_lse
                    line = jnp.where(part == k, here, line)
            tops.append(jnp.where(masks[tile], line, LOW))

        def across(value, op):
            shift = pairs
            while shift < LANES:
                value = op(value, pltpu.roll(value, shift, 1))
                shift *= 2
            return value

        overall = across(functools.reduce(jnp.maximum, tops), jnp.maximum)
        weights = [jnp.where(m, jnp.exp(s - overall), 0.0) for m, s in zip(masks, tops)]
        denom = across(functools.reduce(jnp.add, weights), jnp.add)
        inverse = 1.0 / jnp.where(same, denom, 1.0)
        coef = jnp.concatenate([(w * inverse).astype(BF16) for w in weights], axis=1)

        if compact:
            coef = jnp.dot(coef, order_ref[...], preferred_element_type=F32).astype(BF16)
        return coef

    pair_up = 2

    def lines_of(k):
        return flat_ref[pl.ds(k, lines, stride=heads), :].astype(BF16)

    def project(j, h):
        outs = []
        for k in range(h, h + pair_up):
            left = (
                left_ref[h // pair_up, pl.ds((k - h) * lines, lines), :] if compact else lines_of(k)
            )
            outs.append(
                jnp.dot(
                    left, w_ref[j, pl.ds(k * width, width), :], preferred_element_type=F32
                )
            )
        if compact:
            y_ref[j, pl.ds(h * lines, pair_up * lines), :] = jnp.concatenate(
                outs, axis=0
            ).astype(BF16)
        else:
            for k in range(pair_up):
                for c in range(wide // LANES):
                    y_ref[c, pl.ds(h + k, lines, stride=heads), :] = outs[k][
                        :, c * LANES : (c + 1) * LANES
                    ]

    def mix(j, part):
        if compact:
            right = y_ref[j, :, pl.ds(part * chunk, chunk)]
        else:
            right = jnp.concatenate(
                [y_ref[c].astype(BF16) for c in range(wide // LANES)], axis=1
            )[:, j * half : (j + 1) * half]
        half_ref[j, part] = jnp.dot(coef, right, preferred_element_type=F32)

    for copy in copies_w:
        copy.wait()
    swaps = []
    for piece in range(pieces):
        all_mean[piece].wait_recv()
        for slot in range(ctx_size):
            for t in range(answer_len):
                flat_ref[pl.ds(slot * pairs + t * heads + piece * some, some), :] = mean_all[
                    piece, slot, pl.ds(t * some, some), :
                ].astype(F32)
        here = range(piece * some, (piece + 1) * some, pair_up)
        if piece == 0:
            coef = make_coef()
        for h in here:
            if compact:
                left_ref[h // pair_up] = jnp.concatenate(
                    [lines_of(k) for k in range(h, h + pair_up)], axis=0
                )
            project(0, h)
    for part in range(half // chunk):
        for j in range(1 if compact else head_size):
            mix(j, part)
        copy = pltpu.make_async_remote_copy(
            src_ref=half_ref.at[theirs, part],
            dst_ref=far_half.at[part],
            send_sem=half_sem.at[0, part],
            recv_sem=half_sem.at[1, part],
            device_id=(grp, mine, partner),
            device_id_type=pl.DeviceIdType.MESH,
        )
        copy.start()
        swaps.append(copy)
    if compact:
        for h in range(0, heads, pair_up):
            project(1, h)
        for part in range(half // chunk):
            mix(1, part)
    row_token = lax.rem(iota((rows, chunk), 0), answer_len)
    squared, read, blocks = 0.0, 0.0, []
    for part, copy in enumerate(swaps):
        here = pl.ds(part * chunk, chunk)
        reader = [
            readout_ref[t : t + 1, here].astype(F32) * gain_ref[:, here]
            for t in range(answer_len)
        ]
        reading = jnp.broadcast_to(reader[0], (rows, chunk))
        for t in range(1, answer_len):
            reading = jnp.where(row_token == t, reader[t], reading)
        copy.wait_recv()
        block = (half_ref[ours, part] + far_half[part]).astype(BF16)
        feature = block.astype(F32)
        blocks.append(block)
        squared += jnp.sum(feature * feature, axis=1, keepdims=True)
        read += jnp.sum(feature * reading, axis=1, keepdims=True)
    squares, dotted = to_row(squared), to_row(read)
    me = mine * head_size + core
    stat_all[me] = jnp.concatenate([squares, dotted], axis=0)
    for mask in range(devices - 1, 0, -1):
        copy = pltpu.make_async_remote_copy(
            src_ref=stat_all.at[me],
            dst_ref=stat_all.at[me],
            send_sem=stat_sem.at[0],
            recv_sem=stat_sem.at[1],
            device_id=other(mask),
            device_id_type=pl.DeviceIdType.MESH,
        )
        copy.start()
    all_stat = bytes_of(stat_all.at[pl.ds(0, devices - 1)], stat_sem.at[0], stat_sem.at[1])
    for part, block in enumerate(blocks):
        proj_ref[:, :, pl.ds(part * chunk, chunk)] = (
            block.astype(F32).reshape(ablations, answer_len, chunk).astype(BF16)
        )
    for copy in [all_lse] + all_mean:
        copy.wait_send()
    for copy in swaps:
        copy.wait_send()
    all_stat.wait_recv()
    summary = stat_all[0]
    for i in range(1, devices):
        summary = summary + stat_all[i]
    logits = summary[1:2] * lax.rsqrt(summary[0:1] / features + EPSILON)
    spread = jnp.transpose(jnp.broadcast_to(logits, (LANES, LANES)))
    picked = jnp.where(
        iota((rows, ablations), 0) // answer_len == iota((rows, ablations), 1),
        spread[:, :ablations],
        0.0,
    )
    row_of = lax.rem(iota((rows, ablations), 0), answer_len)
    for t in range(answer_len):
        logit_ref[t : t + 1, :] = jnp.sum(
            jnp.where(row_of == t, picked, 0.0), axis=0, keepdims=True
        )
    target_dev = logits - jnp.sum(logits, axis=1, keepdims=True) / rows
    answer = jnp.sum(solver * target_dev, axis=1, keepdims=True)
    diagonal = iota((sources, sources), 0) == iota((sources, sources), 1)
    attr_ref[...] = jnp.sum(jnp.where(diagonal, answer, 0.0), axis=0, keepdims=True)
    all_stat.wait_send()


def finish(*refs):
    sources, targets, sem = refs[:3], refs[3:6], refs[6]
    stores = [pltpu.make_async_copy(sources[i], targets[i], sem.at[i]) for i in range(3)]
    for copy in stores:
        copy.start()
    for copy in stores:
        copy.wait()


def on_device(
    ctx_size,
    head_size,
    queries,
    keys,
    values,
    new_keys,
    new_values,
    keep,
    block_source,
    out_weight,
    readout,
    gain,
):
    answer_len, heads, width = queries.shape
    tokens, kv_here, _ = keys.shape
    assert tokens == BLOCK
    pairs = answer_len * heads
    ablations, sources = keep.shape
    rows = ablations * answer_len
    depth, columns = out_weight.shape
    half = columns // head_size
    per = LANES // pairs
    assert rows == LANES and per * pairs == LANES and width == LANES
    slots = slot_count(ctx_size, pairs)
    lines = -(-slots * answer_len // 8) * 8
    compact = lines <= 32 and half % LANES == 0
    if not compact:
        lines = slots * answer_len
    devices = ctx_size * head_size
    pieces = 2
    sides = head_size if compact else 1
    chunk = 2 * LANES if half % (2 * LANES) == 0 else half
    parts = half // chunk
    assert head_size == 2
    assert all(size & (size - 1) == 0 for size in (ctx_size, head_size))
    hbm = pl.BlockSpec(memory_space=pltpu.HBM)
    vmem = pl.BlockSpec(memory_space=pltpu.VMEM)
    projected, logits, attribution = pl.pallas_call(
        functools.partial(
            kernel, ctx_size, head_size, answer_len, kv_here, columns * ctx_size
        ),
        out_shape=(
            jax.ShapeDtypeStruct((ablations, answer_len, half), BF16),
            jax.ShapeDtypeStruct((answer_len, ablations), F32),
            jax.ShapeDtypeStruct((1, sources), F32),
        ),
        in_specs=[hbm] * 10,
        out_specs=(vmem, vmem, vmem),
        scratch_shapes=[
            pltpu.SMEM((ctx_size,), jnp.int32),
            pltpu.VMEM((pairs, width), BF16),
            pltpu.VMEM((tokens * kv_here, width), BF16),
            pltpu.VMEM((tokens * kv_here, width), BF16),
            pltpu.VMEM((answer_len * kv_here, width), BF16),
            pltpu.VMEM((answer_len * kv_here, width), BF16),
            pltpu.VMEM((sources, ablations), jnp.int32),
            pltpu.VMEM((sides, depth, columns // sides), BF16),
            pltpu.VMEM((answer_len, half), BF16),
            pltpu.VMEM((1, half), F32),
            pltpu.VMEM((pieces, ctx_size, pairs // pieces, width), BF16),
            pltpu.VMEM((ctx_size, 1, LANES), F32),
            pltpu.VMEM((heads * lines, width), F32),
            pltpu.VMEM((head_size, heads * lines, half), BF16)
            if compact
            else pltpu.VMEM((columns // LANES, heads * lines, LANES), F32),
            pltpu.VMEM((slots * pairs, heads * lines) if compact else (8, LANES), BF16),
            pltpu.VMEM((heads // 2, 2 * lines, width) if compact else (16, LANES), BF16),
            pltpu.VMEM((head_size, parts, rows, chunk), F32),
            pltpu.VMEM((parts, rows, chunk), F32),
            pltpu.VMEM((devices, 2, LANES), F32),
            pltpu.SemaphoreType.DMA((4,)),
            pltpu.SemaphoreType.DMA((sides,)),
            pltpu.SemaphoreType.DMA((2, pieces)),
            pltpu.SemaphoreType.DMA((2,)),
            pltpu.SemaphoreType.DMA((2, parts)),
            pltpu.SemaphoreType.DMA((2,)),
        ],
        compiler_params=pltpu.CompilerParams(
            collective_id=0, has_side_effects=True, vmem_limit_bytes=48 << 20
        ),
        name="attribute",
    )(
        *(pltpu.with_memory_space_constraint(x, pltpu.HBM) for x in (
        block_source,
        queries.reshape(pairs, width),
        keys.reshape(tokens * kv_here, width),
        values.reshape(tokens * kv_here, width),
        new_keys.reshape(-1, width),
        new_values.reshape(-1, width),
        keep.T,
        out_weight,
        readout,
        gain.reshape(1, -1),
        )),
    )
    projected, logits, attribution = pl.pallas_call(
        finish,
        out_shape=(
            jax.ShapeDtypeStruct(projected.shape, BF16),
            jax.ShapeDtypeStruct(logits.shape, F32),
            jax.ShapeDtypeStruct(attribution.shape, F32),
        ),
        in_specs=[vmem] * 3,
        compiler_params=pltpu.CompilerParams(vmem_limit_bytes=1 << 20),
        out_specs=[hbm] * 3,
        scratch_shapes=[pltpu.SemaphoreType.DMA((3,))],
        name="finish",
    )(projected, logits, attribution)
    return projected, logits.T, attribution.reshape(sources)


def solution(mesh):
    in_specs = (
        P("grp", "head", None),
        P(("grp", "ctx"), "head", None),
        P(("grp", "ctx"), "head", None),
        P("grp", "head", None),
        P("grp", "head", None),
        P("grp", None),
        P("grp"),
        P("head", "ctx"),
        P("grp", ("ctx", "head")),
        P(("ctx", "head")),
    )
    out_specs = (P("grp", None, ("ctx", "head")), P("grp", None), P("grp"))
    return jax.shard_map(
        functools.partial(on_device, mesh.shape["ctx"], mesh.shape["head"]),
        mesh=mesh,
        in_specs=in_specs,
        out_specs=out_specs,
        check_vma=False,
    )
```

```python
import functools

import jax
import jax.numpy as jnp
from jax import lax
from jax.experimental import pallas as pl
from jax.experimental.pallas import tpu as pltpu
from jax.sharding import PartitionSpec as P

BLOCK = 512
EPSILON = 1e-05
RIDGE = 1.0
LOW = -1e30
LANES = 128
F32 = jnp.float32
BF16 = jnp.bfloat16
NT = (((1,), (1,)), ((), ()))


def iota(shape, axis):
    return lax.broadcasted_iota(jnp.int32, shape, axis)


def powers(size):
    return [1 << i for i in range(size.bit_length() - 1)]


def slot_count(ctx_size, pairs):
    per = LANES // pairs
    return -(-(ctx_size + 1) // per) * per


def to_row(column):
    return jnp.transpose(jnp.broadcast_to(column, (LANES, LANES)))[0:1, :]


def kernel(
    ctx_size,
    head_size,
    answer_len,
    kv_here,
    bs_hbm,
    q_hbm,
    k_hbm,
    v_hbm,
    nk_hbm,
    nv_hbm,
    keep_hbm,
    w_hbm,
    readout_hbm,
    gain_hbm,
    proj_ref,
    summary_ref,
    solver_ref,
    bs_ref,
    q_ref,
    k_ref,
    v_ref,
    nk_ref,
    nv_ref,
    keep_ref,
    w_ref,
    readout_ref,
    gain_ref,
    mean_all,
    lse_all,
    flat_ref,
    y_ref,
    order_ref,
    left_ref,
    half_ref,
    far_half,
    stat_all,
    local_sem,
    arrive_sem,
    sent_sem,
):
    grp = lax.axis_index("grp")
    mine = lax.axis_index("ctx")
    core = lax.axis_index("head")
    pairs, width = q_ref.shape
    heads = pairs // answer_len
    group = heads // kv_here
    tokens = k_ref.shape[0]
    sources, ablations = keep_ref.shape
    slots = slot_count(ctx_size, pairs)
    lines = flat_ref.shape[0] // pairs * answer_len
    compact = len(left_ref.shape) == 3
    sides, _, wide = w_ref.shape
    half = wide * sides // head_size
    chunk = half_ref.shape[3]
    partner = lax.rem(core + 1, head_size)
    turn = [partner, core]
    theirs, ours = (0, 1) if compact else (partner, core)
    scale = width ** (-0.5)
    rows = ablations * answer_len
    per = LANES // pairs
    devices = ctx_size * head_size

    loads = [
        pltpu.make_async_copy(source, target, local_sem.at[min(max(i, 1), 3) - 1])
        for i, (source, target) in enumerate(
            (
                (q_hbm, q_ref),
                (k_hbm, k_ref),
                (v_hbm, v_ref),
                (nk_hbm, nk_ref),
                (nv_hbm, nv_ref),
                (keep_hbm, keep_ref),
                (bs_hbm, bs_ref),
                (readout_hbm, readout_ref),
                (gain_hbm, gain_ref),
            )
        )
    ]
    for copy in loads:
        copy.start()
    copies_w = [
        pltpu.make_async_copy(
            w_hbm.at[:, pl.ds(pl.multiple_of(turn[j] * half, LANES), half)] if compact else w_hbm,
            w_ref.at[j],
            local_sem.at[3],
        )
        for j in range(sides)
    ]
    for copy in copies_w:
        copy.start()

    def flips(position, size):
        return [bit * (1 - 2 * lax.rem(position // bit, 2)) for bit in powers(size)]

    ctx_flips, core_flips = flips(mine, ctx_size), flips(core, head_size)

    def flipped(position, deltas, mask):
        for i, delta in enumerate(deltas):
            if mask >> i & 1:
                position = position + delta
        return position

    def other(mask):
        return (
            grp,
            flipped(mine, ctx_flips, mask // head_size),
            flipped(core, core_flips, mask % head_size),
        )

    barrier = pltpu.get_barrier_semaphore()
    for mask in range(devices - 1, 0, -1):
        pl.semaphore_signal(
            barrier, inc=1, device_id=other(mask), device_id_type=pl.DeviceIdType.MESH
        )

    loads[0].wait()
    loads[1].wait()
    queries = q_ref[...]
    scores = lax.dot_general(queries, k_ref[...], NT, preferred_element_type=F32) * scale
    near = lax.rem(iota((pairs, tokens), 1), kv_here) == lax.rem(
        iota((pairs, tokens), 0) // group, kv_here
    )
    top = jnp.max(jnp.where(near, scores, LOW), axis=1, keepdims=True)
    expo = jnp.where(near, jnp.exp(scores - top), 0.0)
    total = jnp.sum(expo, axis=1, keepdims=True)
    loads[2].wait()
    summed = jnp.dot(expo.astype(BF16), v_ref[...], preferred_element_type=F32)
    mean = summed / total
    lse = top + jnp.log(total)
    lse_all[mine] = to_row(jnp.concatenate([lse] * per, axis=0))
    pieces = mean_all.shape[0]
    some = heads // pieces
    for piece in range(pieces):
        for t in range(answer_len):
            first = t * heads + piece * some
            mean_all[piece, mine, pl.ds(t * some, some), :] = mean[first : first + some].astype(
                BF16
            )

    pl.semaphore_wait(barrier, devices - 1)

    sent_mean, sent_lse, sent_half, sent_stat = [sent_sem.at[i] for i in range(4)]
    parts = half // chunk
    arrive_mean = [arrive_sem.at[piece] for piece in range(pieces)]
    arrive_half = [arrive_sem.at[pieces + part] for part in range(parts)]
    arrive_stat = arrive_sem.at[pieces + parts]
    arrive_lse = arrive_sem.at[pieces + parts + 1]

    def remote(source, target, send, recv, device):
        return pltpu.make_async_remote_copy(
            src_ref=source,
            dst_ref=target,
            send_sem=send,
            recv_sem=recv,
            device_id=device,
            device_id_type=pl.DeviceIdType.MESH,
        )

    def to_peer(source, send, recv, k):
        place = ctx_size - 1 - k
        peer = jnp.where(place <= mine, place - 1, place)
        remote(source, source, send, recv, (grp, peer, core)).start()

    def bytes_of(block, send, recv):
        return remote(block, block, send, recv, (grp, mine, partner))

    all_lse = bytes_of(lse_all.at[pl.ds(0, ctx_size - 1)], sent_lse, arrive_lse)
    all_mean = [
        bytes_of(mean_all.at[piece, pl.ds(0, ctx_size - 1)], sent_mean, arrive_mean[piece])
        for piece in range(pieces)
    ]

    def send_to(peers, kinds):
        for kind in kinds:
            for k in peers:
                if kind < 0:
                    to_peer(lse_all.at[mine], sent_lse, arrive_lse, k)
                else:
                    to_peer(mean_all.at[kind, mine], sent_mean, arrive_mean[kind], k)

    first = range(1)
    later = range(1, ctx_size - 1)
    send_to(first, range(-1, pieces))
    send_to(later, range(-1, pieces))

    for copy in loads[3:]:
        copy.wait()
    owns = nk_ref.shape[0]
    own_scores = lax.dot_general(queries, nk_ref[...], NT, preferred_element_type=F32) * scale
    place = iota((pairs, owns), 1)
    pair = iota((pairs, owns), 0)
    allowed = (lax.rem(place, kv_here) == lax.rem(pair // group, kv_here)) & (
        place // kv_here <= pair // heads
    )
    own_top = jnp.max(jnp.where(allowed, own_scores, LOW), axis=1, keepdims=True)
    own_expo = jnp.where(allowed, jnp.exp(own_scores - own_top), 0.0)
    own_total = jnp.sum(own_expo, axis=1, keepdims=True)
    own_probs = own_expo.astype(BF16).astype(F32)
    own_values = nv_ref[...].astype(F32)
    own_sum = jnp.zeros((pairs, width), F32)
    for i in range(owns):
        own_sum += own_probs[:, i : i + 1] * own_values[i : i + 1, :]
    flat_ref[pl.ds(ctx_size * pairs, pairs), :] = own_sum / own_total
    for slot in range(ctx_size + 1, flat_ref.shape[0] // pairs):
        flat_ref[pl.ds(slot * pairs, pairs), :] = jnp.zeros((pairs, width), F32)
    own_lse = to_row(jnp.concatenate([own_top + jnp.log(own_total)] * per, axis=0))

    keep = keep_ref[...].astype(F32)
    repeat = (iota((rows, ablations), 0) // answer_len == iota((rows, ablations), 1)).astype(F32)
    keep_rows = lax.dot_general(repeat, keep, NT, preferred_element_type=F32)
    lane = iota((1, LANES), 1)
    part = lane // pairs
    same = lax.rem(iota((rows, LANES), 1), pairs) // heads == lax.rem(
        iota((rows, LANES), 0), answer_len
    )
    masks = []
    for tile in range(slots // per):
        source = jnp.full((1, LANES), -1, jnp.int32)
        own_lane = jnp.zeros((1, LANES), F32)
        for k in range(per):
            slot = tile * per + k
            if slot < ctx_size:
                source = jnp.where(part == k, bs_ref[slot], source)
            if slot == ctx_size:
                own_lane = jnp.where(part == k, 1.0, own_lane)
        chosen = (iota((sources, LANES), 0) == source).astype(F32)
        kept = jnp.dot(keep_rows, chosen, preferred_element_type=F32) + own_lane
        masks.append((kept > 0.5) & same)

    eye = (iota((sources, sources), 0) == iota((sources, sources), 1)).astype(F32)
    keep_cols = lax.dot_general(keep, repeat, NT, preferred_element_type=F32)
    gram = lax.dot_general(keep, keep, NT, preferred_element_type=F32)
    count = jnp.sum(keep, axis=1, keepdims=True)
    count_row = jnp.sum(keep_rows, axis=0, keepdims=True) / answer_len
    system = gram - count * count_row / ablations + RIDGE * eye
    centered = keep_cols - count / ablations

    def sweep(k, state):
        on_row = iota((sources, sources), 0) == k
        on_col = iota((sources, sources), 1) == k
        row = jnp.sum(jnp.where(on_row, state, 0.0), axis=0, keepdims=True)
        col = jnp.sum(jnp.where(on_col, state, 0.0), axis=1, keepdims=True)
        pivot = jnp.sum(jnp.where(on_col[0:1], row, 0.0), axis=1, keepdims=True)
        inverse = 1.0 / pivot
        return jnp.where(
            on_row,
            jnp.where(on_col, -inverse, row * inverse),
            jnp.where(on_col, col * inverse, state - col * (row * inverse)),
        )

    swept = lax.fori_loop(0, sources, sweep, system, unroll=sources <= 8)
    solver_ref[...] = -jnp.dot(swept, centered, precision=lax.Precision.HIGHEST, preferred_element_type=F32)

    if compact:
        spot = iota((1, heads * lines), 1)
        line = lax.rem(spot, lines)
        wanted = (
            line // answer_len * pairs + lax.rem(line, answer_len) * heads + spot // lines
        )
        order_ref[...] = (iota(order_ref.shape, 0) == wanted).astype(BF16)
    all_lse.wait_recv()
    all_mean[0].wait_recv()

    def make_coef():
        tops = []
        for tile in range(slots // per):
            line = jnp.full((1, LANES), LOW, F32)
            for k in range(per):
                slot = tile * per + k
                if slot <= ctx_size:
                    here = lse_all[slot] if slot < ctx_size else own_lse
                    line = jnp.where(part == k, here, line)
            tops.append(jnp.where(masks[tile], line, LOW))

        def across(value, op):
            shift = pairs
            while shift < LANES:
                value = op(value, pltpu.roll(value, shift, 1))
                shift *= 2
            return value

        overall = across(functools.reduce(jnp.maximum, tops), jnp.maximum)
        weights = [jnp.where(m, jnp.exp(s - overall), 0.0) for m, s in zip(masks, tops)]
        denom = across(functools.reduce(jnp.add, weights), jnp.add)
        inverse = 1.0 / jnp.where(same, denom, 1.0)
        coef = jnp.concatenate([(w * inverse).astype(BF16) for w in weights], axis=1)

        if compact:
            coef = jnp.dot(coef, order_ref[...], preferred_element_type=F32).astype(BF16)
        return coef

    pair_up = 2

    def lines_of(k):
        return flat_ref[pl.ds(k, lines, stride=heads), :].astype(BF16)

    def project(j, h):
        outs = []
        for k in range(h, h + pair_up):
            left = (
                left_ref[h // pair_up, pl.ds((k - h) * lines, lines), :] if compact else lines_of(k)
            )
            outs.append(
                jnp.dot(
                    left, w_ref[j, pl.ds(k * width, width), :], preferred_element_type=F32
                )
            )
        if compact:
            y_ref[j, pl.ds(h * lines, pair_up * lines), :] = jnp.concatenate(
                outs, axis=0
            ).astype(BF16)
        else:
            for k in range(pair_up):
                for c in range(wide // LANES):
                    y_ref[c, pl.ds(h + k, lines, stride=heads), :] = outs[k][
                        :, c * LANES : (c + 1) * LANES
                    ]

    def mix(j, part):
        if compact:
            right = y_ref[j, :, pl.ds(part * chunk, chunk)]
        else:
            right = jnp.concatenate(
                [y_ref[c].astype(BF16) for c in range(wide // LANES)], axis=1
            )[:, j * half : (j + 1) * half]
        half_ref[j, part] = jnp.dot(coef, right, preferred_element_type=F32)

    for copy in copies_w:
        copy.wait()
    swaps = []
    for piece in range(pieces):
        if piece:
            all_mean[piece].wait_recv()
        for slot in range(ctx_size):
            for t in range(answer_len):
                flat_ref[pl.ds(slot * pairs + t * heads + piece * some, some), :] = mean_all[
                    piece, slot, pl.ds(t * some, some), :
                ].astype(F32)
        here = range(piece * some, (piece + 1) * some, pair_up)
        if piece == 0:
            coef = make_coef()
        for h in here:
            if compact:
                left_ref[h // pair_up] = jnp.concatenate(
                    [lines_of(k) for k in range(h, h + pair_up)], axis=0
                )
            project(0, h)
    for part in range(half // chunk):
        for j in range(1 if compact else head_size):
            mix(j, part)
        copy = remote(
            half_ref.at[theirs, part],
            far_half.at[part],
            sent_half,
            arrive_half[part],
            (grp, mine, partner),
        )
        copy.start()
        swaps.append(copy)
    if compact:
        for h in range(0, heads, pair_up):
            project(1, h)
        for part in range(half // chunk):
            mix(1, part)
    row_token = lax.rem(iota((rows, chunk), 0), answer_len)
    squared, read, blocks = 0.0, 0.0, []
    for part, copy in enumerate(swaps):
        here = pl.ds(part * chunk, chunk)
        reader = [
            readout_ref[t : t + 1, here].astype(F32) * gain_ref[:, here]
            for t in range(answer_len)
        ]
        reading = jnp.broadcast_to(reader[0], (rows, chunk))
        for t in range(1, answer_len):
            reading = jnp.where(row_token == t, reader[t], reading)
        copy.wait_recv()
        block = (half_ref[ours, part] + far_half[part]).astype(BF16)
        feature = block.astype(F32)
        blocks.append(block)
        squared += jnp.sum(feature * feature, axis=1, keepdims=True)
        read += jnp.sum(feature * reading, axis=1, keepdims=True)
    squares, dotted = to_row(squared), to_row(read)
    me = mine * head_size + core
    stat_all[me] = jnp.concatenate([squares, dotted], axis=0)
    for mask in range(devices - 1, 0, -1):
        remote(stat_all.at[me], stat_all.at[me], sent_stat, arrive_stat, other(mask)).start()
    all_stat = bytes_of(stat_all.at[pl.ds(0, devices - 1)], sent_stat, arrive_stat)
    for part, block in enumerate(blocks):
        proj_ref[:, :, pl.ds(part * chunk, chunk)] = (
            block.astype(F32).reshape(ablations, answer_len, chunk).astype(BF16)
        )
    all_stat.wait_recv()
    summary = stat_all[0]
    for i in range(1, devices):
        summary = summary + stat_all[i]
    summary_ref[...] = summary
    for copy in (
        all_lse,
        bytes_of(mean_all.at[:, pl.ds(0, ctx_size - 1)], sent_mean, arrive_lse),
        bytes_of(far_half, sent_half, arrive_lse),
        all_stat,
    ):
        copy.wait_send()


def finish(
    answer_len,
    features,
    proj_ref,
    summary_ref,
    solver_ref,
    proj_out,
    logit_out,
    attr_out,
    logit_ref,
    attr_ref,
    sem,
):
    ablations = proj_ref.shape[0]
    sources = solver_ref.shape[0]
    rows = ablations * answer_len
    stores = [pltpu.make_async_copy(proj_ref, proj_out, sem.at[0])]
    stores[0].start()
    summary, solver = summary_ref[...], solver_ref[...]
    logits = summary[1:2] * lax.rsqrt(summary[0:1] / features + EPSILON)
    spread = jnp.transpose(jnp.broadcast_to(logits, (LANES, LANES)))
    picked = jnp.where(
        iota((rows, ablations), 0) // answer_len == iota((rows, ablations), 1),
        spread[:, :ablations],
        0.0,
    )
    row_of = lax.rem(iota((rows, ablations), 0), answer_len)
    for t in range(answer_len):
        logit_ref[t : t + 1, :] = jnp.sum(
            jnp.where(row_of == t, picked, 0.0), axis=0, keepdims=True
        )
    target_dev = logits - jnp.sum(logits, axis=1, keepdims=True) / rows
    answer = jnp.sum(solver * target_dev, axis=1, keepdims=True)
    diagonal = iota((sources, sources), 0) == iota((sources, sources), 1)
    attr_ref[...] = jnp.sum(jnp.where(diagonal, answer, 0.0), axis=0, keepdims=True)
    stores.append(pltpu.make_async_copy(logit_ref, logit_out, sem.at[0]))
    stores.append(pltpu.make_async_copy(attr_ref, attr_out, sem.at[0]))
    for copy in stores[1:]:
        copy.start()
    for copy in stores:
        copy.wait()


def on_device(
    ctx_size,
    head_size,
    queries,
    keys,
    values,
    new_keys,
    new_values,
    keep,
    block_source,
    out_weight,
    readout,
    gain,
):
    answer_len, heads, width = queries.shape
    tokens, kv_here, _ = keys.shape
    assert tokens == BLOCK
    pairs = answer_len * heads
    ablations, sources = keep.shape
    rows = ablations * answer_len
    depth, columns = out_weight.shape
    half = columns // head_size
    per = LANES // pairs
    assert rows == LANES and per * pairs == LANES and width == LANES
    slots = slot_count(ctx_size, pairs)
    lines = -(-slots * answer_len // 8) * 8
    compact = lines <= 32 and half % LANES == 0
    if not compact:
        lines = slots * answer_len
    devices = ctx_size * head_size
    pieces = 2
    sides = head_size if compact else 1
    chunk = half
    parts = half // chunk
    assert head_size == 2
    assert all(size & (size - 1) == 0 for size in (ctx_size, head_size))
    hbm = pl.BlockSpec(memory_space=pltpu.HBM)
    vmem = pl.BlockSpec(memory_space=pltpu.VMEM)
    projected, summary, solver = pl.pallas_call(
        functools.partial(kernel, ctx_size, head_size, answer_len, kv_here),
        out_shape=(
            jax.ShapeDtypeStruct((ablations, answer_len, half), BF16),
            jax.ShapeDtypeStruct((2, rows), F32),
            jax.ShapeDtypeStruct((sources, rows), F32),
        ),
        in_specs=[hbm] * 10,
        out_specs=(vmem, vmem, vmem),
        scratch_shapes=[
            pltpu.SMEM((ctx_size,), jnp.int32),
            pltpu.VMEM((pairs, width), BF16),
            pltpu.VMEM((tokens * kv_here, width), BF16),
            pltpu.VMEM((tokens * kv_here, width), BF16),
            pltpu.VMEM((answer_len * kv_here, width), BF16),
            pltpu.VMEM((answer_len * kv_here, width), BF16),
            pltpu.VMEM((sources, ablations), jnp.int32),
            pltpu.VMEM((sides, depth, columns // sides), BF16),
            pltpu.VMEM((answer_len, half), BF16),
            pltpu.VMEM((1, half), F32),
            pltpu.VMEM((pieces, ctx_size, pairs // pieces, width), BF16),
            pltpu.VMEM((ctx_size, 1, LANES), F32),
            pltpu.VMEM((heads * lines, width), F32),
            pltpu.VMEM((head_size, heads * lines, half), BF16)
            if compact
            else pltpu.VMEM((columns // LANES, heads * lines, LANES), F32),
            pltpu.VMEM((slots * pairs, heads * lines) if compact else (8, LANES), BF16),
            pltpu.VMEM((heads // 2, 2 * lines, width) if compact else (16, LANES), BF16),
            pltpu.VMEM((head_size, parts, rows, chunk), F32),
            pltpu.VMEM((parts, rows, chunk), F32),
            pltpu.VMEM((devices, 2, LANES), F32),
            pltpu.SemaphoreType.DMA((4,)),
            pltpu.SemaphoreType.DMA((pieces + parts + 2,)),
            pltpu.SemaphoreType.DMA((4,)),
        ],
        compiler_params=pltpu.CompilerParams(
            collective_id=0, has_side_effects=True, vmem_limit_bytes=48 << 20
        ),
        name="attribute",
    )(
        *(pltpu.with_memory_space_constraint(x, pltpu.HBM) for x in (
        block_source,
        queries.reshape(pairs, width),
        keys.reshape(tokens * kv_here, width),
        values.reshape(tokens * kv_here, width),
        new_keys.reshape(-1, width),
        new_values.reshape(-1, width),
        keep.T,
        out_weight,
        readout,
        gain.reshape(1, -1),
        )),
    )
    projected, logits, attribution = pl.pallas_call(
        functools.partial(finish, answer_len, columns * ctx_size),
        out_shape=(
            jax.ShapeDtypeStruct(projected.shape, BF16),
            jax.ShapeDtypeStruct((answer_len, ablations), F32),
            jax.ShapeDtypeStruct((1, sources), F32),
        ),
        in_specs=[vmem] * 3,
        compiler_params=pltpu.CompilerParams(vmem_limit_bytes=2 << 20),
        out_specs=[hbm] * 3,
        scratch_shapes=[
            pltpu.VMEM((answer_len, ablations), F32),
            pltpu.VMEM((1, sources), F32),
            pltpu.SemaphoreType.DMA((1,)),
        ],
        name="finish",
    )(projected, summary, solver)
    return projected, logits.T, attribution.reshape(sources)


def solution(mesh):
    in_specs = (
        P("grp", "head", None),
        P(("grp", "ctx"), "head", None),
        P(("grp", "ctx"), "head", None),
        P("grp", "head", None),
        P("grp", "head", None),
        P("grp", None),
        P("grp"),
        P("head", "ctx"),
        P("grp", ("ctx", "head")),
        P(("ctx", "head")),
    )
    out_specs = (P("grp", None, ("ctx", "head")), P("grp", None), P("grp"))
    return jax.shard_map(
        functools.partial(on_device, mesh.shape["ctx"], mesh.shape["head"]),
        mesh=mesh,
        in_specs=in_specs,
        out_specs=out_specs,
        check_vma=False,
    )
```

```python
import functools

import jax
import jax.numpy as jnp
from jax import lax
from jax.experimental import pallas as pl
from jax.experimental.pallas import tpu as pltpu
from jax.sharding import PartitionSpec as P

BLOCK = 512
EPSILON = 1e-05
RIDGE = 1.0
LOW = -1e30
LANES = 128
F32 = jnp.float32
BF16 = jnp.bfloat16
NT = (((1,), (1,)), ((), ()))


def iota(shape, axis):
    return lax.broadcasted_iota(jnp.int32, shape, axis)


def powers(size):
    return [1 << i for i in range(size.bit_length() - 1)]


def slot_count(ctx_size, pairs):
    per = LANES // pairs
    return -(-(ctx_size + 1) // per) * per


def to_row(column):
    return jnp.transpose(jnp.broadcast_to(column, (LANES, LANES)))[0:1, :]


def fold(block):
    step = min(block.shape[1], LANES)
    return sum(block[:, i : i + step] for i in range(0, block.shape[1], step))


def row_sums(block):
    if block.shape[1] < LANES:
        return to_row(jnp.sum(block, axis=1, keepdims=True))
    return jnp.sum(jnp.transpose(block), axis=0, keepdims=True)


def kernel(
    ctx_size,
    head_size,
    answer_len,
    kv_here,
    bs_hbm,
    q_hbm,
    k_hbm,
    v_hbm,
    nk_hbm,
    nv_hbm,
    keep_hbm,
    w_hbm,
    readout_hbm,
    gain_hbm,
    proj_ref,
    summary_ref,
    solver_ref,
    bs_ref,
    q_ref,
    k_ref,
    v_ref,
    nk_ref,
    nv_ref,
    keep_ref,
    w_ref,
    readout_ref,
    gain_ref,
    mean_all,
    lse_all,
    flat_ref,
    y_ref,
    order_ref,
    left_ref,
    half_ref,
    far_half,
    sum_ref,
    stat_all,
    local_sem,
    arrive_sem,
    sent_sem,
):
    grp = lax.axis_index("grp")
    mine = lax.axis_index("ctx")
    core = lax.axis_index("head")
    pairs, width = q_ref.shape
    heads = pairs // answer_len
    group = heads // kv_here
    tokens = k_ref.shape[0]
    sources, ablations = keep_ref.shape
    slots = slot_count(ctx_size, pairs)
    lines = flat_ref.shape[0] // pairs * answer_len
    compact = len(left_ref.shape) == 3
    sides, _, wide = w_ref.shape
    half = wide * sides // head_size
    chunk = half_ref.shape[3]
    partner = lax.rem(core + 1, head_size)
    turn = [partner, core]
    theirs, ours = (0, 1) if compact else (partner, core)
    scale = width ** (-0.5)
    rows = ablations * answer_len
    per = LANES // pairs
    devices = ctx_size * head_size

    def flips(position, size):
        return [bit * (1 - 2 * lax.rem(position // bit, 2)) for bit in powers(size)]

    ctx_flips, core_flips = flips(mine, ctx_size), flips(core, head_size)

    def flipped(position, deltas, mask):
        for i, delta in enumerate(deltas):
            if mask >> i & 1:
                position = position + delta
        return position

    def other(mask):
        return (
            grp,
            flipped(mine, ctx_flips, mask // head_size),
            flipped(core, core_flips, mask % head_size),
        )

    barrier = pltpu.get_barrier_semaphore()
    for mask in range(devices - 1, 0, -1):
        pl.semaphore_signal(
            barrier, inc=1, device_id=other(mask), device_id_type=pl.DeviceIdType.MESH
        )

    loads = [
        pltpu.make_async_copy(source, target, local_sem.at[min(max(i, 1), 3) - 1])
        for i, (source, target) in enumerate(
            (
                (q_hbm, q_ref),
                (k_hbm, k_ref),
                (v_hbm, v_ref),
                (nk_hbm, nk_ref),
                (nv_hbm, nv_ref),
                (keep_hbm, keep_ref),
                (bs_hbm, bs_ref),
                (readout_hbm, readout_ref),
                (gain_hbm, gain_ref),
            )
        )
    ]
    for copy in loads:
        copy.start()
    copies_w = [
        pltpu.make_async_copy(
            w_hbm.at[:, pl.ds(pl.multiple_of(turn[j] * half, LANES), half)] if compact else w_hbm,
            w_ref.at[j],
            local_sem.at[3],
        )
        for j in range(sides)
    ]
    for copy in copies_w:
        copy.start()

    loads[0].wait()
    loads[1].wait()
    queries = q_ref[...]
    scores = lax.dot_general(queries, k_ref[...], NT, preferred_element_type=F32) * scale
    near = lax.rem(iota((pairs, tokens), 1), kv_here) == lax.rem(
        iota((pairs, tokens), 0) // group, kv_here
    )
    top = jnp.max(jnp.where(near, scores, LOW), axis=1, keepdims=True)
    expo = jnp.where(near, jnp.exp(scores - top), 0.0)
    total = jnp.sum(expo, axis=1, keepdims=True)
    loads[2].wait()
    summed = jnp.dot(expo.astype(BF16), v_ref[...], preferred_element_type=F32)
    mean = summed / total
    lse = top + jnp.log(total)
    lse_all[mine] = to_row(jnp.concatenate([lse] * per, axis=0))
    pieces = mean_all.shape[0]
    some = heads // pieces
    for piece in range(pieces):
        for t in range(answer_len):
            first = t * heads + piece * some
            mean_all[piece, mine, pl.ds(t * some, some), :] = mean[first : first + some].astype(
                BF16
            )

    pl.semaphore_wait(barrier, devices - 1)

    sent_mean, sent_lse, sent_half, sent_stat = [sent_sem.at[i] for i in range(4)]
    parts = half // chunk
    arrive_mean = [arrive_sem.at[piece] for piece in range(pieces)]
    arrive_half = [arrive_sem.at[pieces + part] for part in range(parts)]
    arrive_stat = arrive_sem.at[pieces + parts]
    arrive_lse = arrive_sem.at[pieces + parts + 1]

    def remote(source, target, send, recv, device):
        return pltpu.make_async_remote_copy(
            src_ref=source,
            dst_ref=target,
            send_sem=send,
            recv_sem=recv,
            device_id=device,
            device_id_type=pl.DeviceIdType.MESH,
        )

    def to_peer(source, send, recv, k):
        place = ctx_size - 1 - k
        peer = jnp.where(place <= mine, place - 1, place)
        remote(source, source, send, recv, (grp, peer, core)).start()

    def bytes_of(block, send, recv):
        return remote(block, block, send, recv, (grp, mine, partner))

    all_lse = bytes_of(lse_all.at[pl.ds(0, ctx_size - 1)], sent_lse, arrive_lse)
    all_mean = [
        bytes_of(mean_all.at[piece, pl.ds(0, ctx_size - 1)], sent_mean, arrive_mean[piece])
        for piece in range(pieces)
    ]

    def send_to(peers, kinds):
        for kind in kinds:
            for k in peers:
                if kind < 0:
                    to_peer(lse_all.at[mine], sent_lse, arrive_lse, k)
                else:
                    to_peer(mean_all.at[kind, mine], sent_mean, arrive_mean[kind], k)

    first = range(1)
    later = range(1, ctx_size - 1)
    send_to(first, range(-1, pieces))
    send_to(later, range(-1, pieces))

    for copy in loads[3:]:
        copy.wait()
    owns = nk_ref.shape[0]
    own_scores = lax.dot_general(queries, nk_ref[...], NT, preferred_element_type=F32) * scale
    place = iota((pairs, owns), 1)
    pair = iota((pairs, owns), 0)
    allowed = (lax.rem(place, kv_here) == lax.rem(pair // group, kv_here)) & (
        place // kv_here <= pair // heads
    )
    own_top = jnp.max(jnp.where(allowed, own_scores, LOW), axis=1, keepdims=True)
    own_expo = jnp.where(allowed, jnp.exp(own_scores - own_top), 0.0)
    own_total = jnp.sum(own_expo, axis=1, keepdims=True)
    own_probs = own_expo.astype(BF16).astype(F32)
    own_values = nv_ref[...].astype(F32)
    own_sum = jnp.zeros((pairs, width), F32)
    for i in range(owns):
        own_sum += own_probs[:, i : i + 1] * own_values[i : i + 1, :]
    flat_ref[pl.ds(ctx_size * pairs, pairs), :] = own_sum / own_total
    for slot in range(ctx_size + 1, flat_ref.shape[0] // pairs):
        flat_ref[pl.ds(slot * pairs, pairs), :] = jnp.zeros((pairs, width), F32)
    own_lse = to_row(jnp.concatenate([own_top + jnp.log(own_total)] * per, axis=0))

    keep = keep_ref[...].astype(F32)
    repeat = (iota((rows, ablations), 0) // answer_len == iota((rows, ablations), 1)).astype(F32)
    keep_rows = lax.dot_general(repeat, keep, NT, preferred_element_type=F32)
    lane = iota((1, LANES), 1)
    part = lane // pairs
    same = lax.rem(iota((rows, LANES), 1), pairs) // heads == lax.rem(
        iota((rows, LANES), 0), answer_len
    )
    masks = []
    for tile in range(slots // per):
        source = jnp.full((1, LANES), -1, jnp.int32)
        own_lane = jnp.zeros((1, LANES), F32)
        for k in range(per):
            slot = tile * per + k
            if slot < ctx_size:
                source = jnp.where(part == k, bs_ref[slot], source)
            if slot == ctx_size:
                own_lane = jnp.where(part == k, 1.0, own_lane)
        chosen = (iota((sources, LANES), 0) == source).astype(F32)
        kept = jnp.dot(keep_rows, chosen, preferred_element_type=F32) + own_lane
        masks.append((kept > 0.5) & same)

    eye = (iota((sources, sources), 0) == iota((sources, sources), 1)).astype(F32)
    keep_cols = lax.dot_general(keep, repeat, NT, preferred_element_type=F32)
    gram = lax.dot_general(keep, keep, NT, preferred_element_type=F32)
    count = jnp.sum(keep, axis=1, keepdims=True)
    count_row = jnp.sum(keep_rows, axis=0, keepdims=True) / answer_len
    system = gram - count * count_row / ablations + RIDGE * eye
    centered = keep_cols - count / ablations

    def sweep(k, state):
        on_row = iota((sources, sources), 0) == k
        on_col = iota((sources, sources), 1) == k
        row = jnp.sum(jnp.where(on_row, state, 0.0), axis=0, keepdims=True)
        col = jnp.sum(jnp.where(on_col, state, 0.0), axis=1, keepdims=True)
        pivot = jnp.sum(jnp.where(on_col[0:1], row, 0.0), axis=1, keepdims=True)
        inverse = 1.0 / pivot
        return jnp.where(
            on_row,
            jnp.where(on_col, -inverse, row * inverse),
            jnp.where(on_col, col * inverse, state - col * (row * inverse)),
        )

    swept = lax.fori_loop(0, sources, sweep, system, unroll=sources <= 8)
    solver_ref[...] = -jnp.dot(swept, centered, precision=lax.Precision.HIGHEST, preferred_element_type=F32)

    if compact:
        spot = iota((1, heads * lines), 1)
        line = lax.rem(spot, lines)
        wanted = (
            line // answer_len * pairs + lax.rem(line, answer_len) * heads + spot // lines
        )
        order_ref[...] = (iota(order_ref.shape, 0) == wanted).astype(BF16)
    all_lse.wait_recv()
    all_mean[0].wait_recv()

    def make_coef():
        tops = []
        for tile in range(slots // per):
            line = jnp.full((1, LANES), LOW, F32)
            for k in range(per):
                slot = tile * per + k
                if slot <= ctx_size:
                    here = lse_all[slot] if slot < ctx_size else own_lse
                    line = jnp.where(part == k, here, line)
            tops.append(jnp.where(masks[tile], line, LOW))

        def across(value, op):
            shift = pairs
            while shift < LANES:
                value = op(value, pltpu.roll(value, shift, 1))
                shift *= 2
            return value

        overall = across(functools.reduce(jnp.maximum, tops), jnp.maximum)
        weights = [jnp.where(m, jnp.exp(s - overall), 0.0) for m, s in zip(masks, tops)]
        denom = across(functools.reduce(jnp.add, weights), jnp.add)
        inverse = 1.0 / jnp.where(same, denom, 1.0)
        coef = jnp.concatenate([(w * inverse).astype(BF16) for w in weights], axis=1)

        if compact:
            coef = jnp.dot(coef, order_ref[...], preferred_element_type=F32).astype(BF16)
        return coef

    pair_up = 2

    def lines_of(k):
        return flat_ref[pl.ds(k, lines, stride=heads), :].astype(BF16)

    def project(j, h):
        outs = []
        for k in range(h, h + pair_up):
            left = (
                left_ref[h // pair_up, pl.ds((k - h) * lines, lines), :] if compact else lines_of(k)
            )
            outs.append(
                jnp.dot(
                    left, w_ref[j, pl.ds(k * width, width), :], preferred_element_type=F32
                )
            )
        if compact:
            y_ref[j, pl.ds(h * lines, pair_up * lines), :] = jnp.concatenate(
                outs, axis=0
            ).astype(BF16)
        else:
            for k in range(pair_up):
                for c in range(wide // LANES):
                    y_ref[c, pl.ds(h + k, lines, stride=heads), :] = outs[k][
                        :, c * LANES : (c + 1) * LANES
                    ]

    def mix(j, part):
        if compact:
            right = y_ref[j, :, pl.ds(part * chunk, chunk)]
        else:
            right = jnp.concatenate(
                [y_ref[c].astype(BF16) for c in range(wide // LANES)], axis=1
            )[:, j * half : (j + 1) * half]
        half_ref[j, part] = jnp.dot(coef, right, preferred_element_type=F32)

    for copy in copies_w:
        copy.wait()
    swaps = []
    for piece in range(pieces):
        if piece:
            all_mean[piece].wait_recv()
        for slot in range(ctx_size):
            for t in range(answer_len):
                flat_ref[pl.ds(slot * pairs + t * heads + piece * some, some), :] = mean_all[
                    piece, slot, pl.ds(t * some, some), :
                ].astype(F32)
        here = range(piece * some, (piece + 1) * some, pair_up)
        if piece == 0:
            coef = make_coef()
        for h in here:
            if compact:
                left_ref[h // pair_up] = jnp.concatenate(
                    [lines_of(k) for k in range(h, h + pair_up)], axis=0
                )
            project(0, h)
    for part in range(half // chunk):
        for j in range(1 if compact else head_size):
            mix(j, part)
        copy = remote(
            half_ref.at[theirs, part],
            far_half.at[part],
            sent_half,
            arrive_half[part],
            (grp, mine, partner),
        )
        copy.start()
        swaps.append(copy)
    if compact:
        for h in range(0, heads, pair_up):
            project(1, h)
        for part in range(half // chunk):
            mix(1, part)
    row_token = lax.rem(iota((rows, chunk), 0), answer_len)
    squared, read = 0.0, 0.0
    for part, copy in enumerate(swaps):
        here = pl.ds(part * chunk, chunk)
        reader = [
            readout_ref[t : t + 1, here].astype(F32) * gain_ref[:, here]
            for t in range(answer_len)
        ]
        reading = jnp.broadcast_to(reader[0], (rows, chunk))
        for t in range(1, answer_len):
            reading = jnp.where(row_token == t, reader[t], reading)
        copy.wait_recv()
        block = (half_ref[ours, part] + far_half[part]).astype(BF16)
        feature = block.astype(F32)
        sum_ref[part] = block
        squared += fold(feature * feature)
        read += fold(feature * reading)
    squares, dotted = row_sums(squared), row_sums(read)
    me = mine * head_size + core
    stat_all[me] = jnp.concatenate([squares, dotted], axis=0)
    for mask in range(devices - 1, 0, -1):
        remote(stat_all.at[me], stat_all.at[me], sent_stat, arrive_stat, other(mask)).start()
    all_stat = bytes_of(stat_all.at[pl.ds(0, devices - 1)], sent_stat, arrive_stat)
    all_lse.wait_send()
    for part in range(parts):
        proj_ref[:, :, pl.ds(part * chunk, chunk)] = (
            sum_ref[part].astype(F32).reshape(ablations, answer_len, chunk).astype(BF16)
        )
    all_stat.wait_recv()
    summary = stat_all[0]
    for i in range(1, devices):
        summary = summary + stat_all[i]
    summary_ref[...] = summary
    for copy in (
        bytes_of(mean_all.at[:, pl.ds(0, ctx_size - 1)], sent_mean, arrive_lse),
        bytes_of(far_half, sent_half, arrive_lse),
        all_stat,
    ):
        copy.wait_send()


def finish(
    answer_len,
    features,
    proj_ref,
    summary_ref,
    solver_ref,
    proj_out,
    logit_out,
    attr_out,
    logit_ref,
    attr_ref,
    sem,
):
    ablations = proj_ref.shape[0]
    sources = solver_ref.shape[0]
    rows = ablations * answer_len
    stores = [pltpu.make_async_copy(proj_ref, proj_out, sem.at[0])]
    stores[0].start()
    summary, solver = summary_ref[...], solver_ref[...]
    logits = summary[1:2] * lax.rsqrt(summary[0:1] / features + EPSILON)
    spread = jnp.transpose(jnp.broadcast_to(logits, (LANES, LANES)))
    picked = jnp.where(
        iota((rows, ablations), 0) // answer_len == iota((rows, ablations), 1),
        spread[:, :ablations],
        0.0,
    )
    row_of = lax.rem(iota((rows, ablations), 0), answer_len)
    for t in range(answer_len):
        logit_ref[t : t + 1, :] = jnp.sum(
            jnp.where(row_of == t, picked, 0.0), axis=0, keepdims=True
        )
    target_dev = logits - jnp.sum(logits, axis=1, keepdims=True) / rows
    answer = jnp.sum(solver * target_dev, axis=1, keepdims=True)
    diagonal = iota((sources, sources), 0) == iota((sources, sources), 1)
    attr_ref[...] = jnp.sum(jnp.where(diagonal, answer, 0.0), axis=0, keepdims=True)
    stores.append(pltpu.make_async_copy(logit_ref, logit_out, sem.at[0]))
    stores.append(pltpu.make_async_copy(attr_ref, attr_out, sem.at[0]))
    for copy in stores[1:]:
        copy.start()
    for copy in stores:
        copy.wait()


def on_device(
    ctx_size,
    head_size,
    queries,
    keys,
    values,
    new_keys,
    new_values,
    keep,
    block_source,
    out_weight,
    readout,
    gain,
):
    answer_len, heads, width = queries.shape
    tokens, kv_here, _ = keys.shape
    assert tokens == BLOCK
    pairs = answer_len * heads
    ablations, sources = keep.shape
    rows = ablations * answer_len
    depth, columns = out_weight.shape
    half = columns // head_size
    per = LANES // pairs
    assert rows == LANES and per * pairs == LANES and width == LANES
    slots = slot_count(ctx_size, pairs)
    lines = -(-slots * answer_len // 8) * 8
    compact = lines <= 32 and half % LANES == 0
    if not compact:
        lines = slots * answer_len
    devices = ctx_size * head_size
    pieces = 2
    sides = head_size if compact else 1
    chunk = half
    parts = half // chunk
    assert head_size == 2
    assert all(size & (size - 1) == 0 for size in (ctx_size, head_size))
    hbm = pl.BlockSpec(memory_space=pltpu.HBM)
    vmem = pl.BlockSpec(memory_space=pltpu.VMEM)
    projected, summary, solver = pl.pallas_call(
        functools.partial(kernel, ctx_size, head_size, answer_len, kv_here),
        out_shape=(
            jax.ShapeDtypeStruct((ablations, answer_len, half), BF16),
            jax.ShapeDtypeStruct((2, rows), F32),
            jax.ShapeDtypeStruct((sources, rows), F32),
        ),
        in_specs=[hbm] * 10,
        out_specs=(vmem, vmem, vmem),
        scratch_shapes=[
            pltpu.SMEM((ctx_size,), jnp.int32),
            pltpu.VMEM((pairs, width), BF16),
            pltpu.VMEM((tokens * kv_here, width), BF16),
            pltpu.VMEM((tokens * kv_here, width), BF16),
            pltpu.VMEM((answer_len * kv_here, width), BF16),
            pltpu.VMEM((answer_len * kv_here, width), BF16),
            pltpu.VMEM((sources, ablations), jnp.int32),
            pltpu.VMEM((sides, depth, columns // sides), BF16),
            pltpu.VMEM((answer_len, half), BF16),
            pltpu.VMEM((1, half), F32),
            pltpu.VMEM((pieces, ctx_size, pairs // pieces, width), BF16),
            pltpu.VMEM((ctx_size, 1, LANES), F32),
            pltpu.VMEM((heads * lines, width), F32),
            pltpu.VMEM((head_size, heads * lines, half), BF16)
            if compact
            else pltpu.VMEM((columns // LANES, heads * lines, LANES), F32),
            pltpu.VMEM((slots * pairs, heads * lines) if compact else (8, LANES), BF16),
            pltpu.VMEM((heads // 2, 2 * lines, width) if compact else (16, LANES), BF16),
            pltpu.VMEM((head_size, parts, rows, chunk), F32),
            pltpu.VMEM((parts, rows, chunk), F32),
            pltpu.VMEM((parts, rows, chunk), BF16),
            pltpu.VMEM((devices, 2, LANES), F32),
            pltpu.SemaphoreType.DMA((4,)),
            pltpu.SemaphoreType.DMA((pieces + parts + 2,)),
            pltpu.SemaphoreType.DMA((4,)),
        ],
        compiler_params=pltpu.CompilerParams(
            collective_id=0, has_side_effects=True, vmem_limit_bytes=48 << 20
        ),
        name="attribute",
    )(
        *(pltpu.with_memory_space_constraint(x, pltpu.HBM) for x in (
        block_source,
        queries.reshape(pairs, width),
        keys.reshape(tokens * kv_here, width),
        values.reshape(tokens * kv_here, width),
        new_keys.reshape(-1, width),
        new_values.reshape(-1, width),
        keep.T,
        out_weight,
        readout,
        gain.reshape(1, -1),
        )),
    )
    projected, logits, attribution = pl.pallas_call(
        functools.partial(finish, answer_len, columns * ctx_size),
        out_shape=(
            jax.ShapeDtypeStruct(projected.shape, BF16),
            jax.ShapeDtypeStruct((answer_len, ablations), F32),
            jax.ShapeDtypeStruct((1, sources), F32),
        ),
        in_specs=[vmem] * 3,
        compiler_params=pltpu.CompilerParams(vmem_limit_bytes=2 << 20),
        out_specs=[hbm] * 3,
        scratch_shapes=[
            pltpu.VMEM((answer_len, ablations), F32),
            pltpu.VMEM((1, sources), F32),
            pltpu.SemaphoreType.DMA((1,)),
        ],
        name="finish",
    )(projected, summary, solver)
    return projected, logits.T, attribution.reshape(sources)


def solution(mesh):
    in_specs = (
        P("grp", "head", None),
        P(("grp", "ctx"), "head", None),
        P(("grp", "ctx"), "head", None),
        P("grp", "head", None),
        P("grp", "head", None),
        P("grp", None),
        P("grp"),
        P("head", "ctx"),
        P("grp", ("ctx", "head")),
        P(("ctx", "head")),
    )
    out_specs = (P("grp", None, ("ctx", "head")), P("grp", None), P("grp"))
    return jax.shard_map(
        functools.partial(on_device, mesh.shape["ctx"], mesh.shape["head"]),
        mesh=mesh,
        in_specs=in_specs,
        out_specs=out_specs,
        check_vma=False,
    )
```

```python
import functools

import jax
import jax.numpy as jnp
from jax import lax
from jax.experimental import pallas as pl
from jax.experimental.pallas import tpu as pltpu
from jax.sharding import PartitionSpec as P

BLOCK = 512
EPSILON = 1e-05
RIDGE = 1.0
LOW = -1e30
LANES = 128
F32 = jnp.float32
BF16 = jnp.bfloat16
NT = (((1,), (1,)), ((), ()))


def iota(shape, axis):
    return lax.broadcasted_iota(jnp.int32, shape, axis)


def powers(size):
    return [1 << i for i in range(size.bit_length() - 1)]


def slot_count(ctx_size, pairs):
    per = LANES // pairs
    return -(-(ctx_size + 1) // per) * per


def to_row(column):
    return jnp.transpose(jnp.broadcast_to(column, (LANES, LANES)))[0:1, :]


def fold(block):
    step = min(block.shape[1], LANES)
    return sum(block[:, i : i + step] for i in range(0, block.shape[1], step))


def row_sums(block):
    if block.shape[1] < LANES:
        return to_row(jnp.sum(block, axis=1, keepdims=True))
    return jnp.sum(jnp.transpose(block), axis=0, keepdims=True)


def kernel(
    ctx_size,
    head_size,
    answer_len,
    kv_here,
    bs_hbm,
    q_hbm,
    k_hbm,
    v_hbm,
    nk_hbm,
    nv_hbm,
    keep_hbm,
    w_hbm,
    readout_hbm,
    gain_hbm,
    proj_ref,
    summary_ref,
    solver_ref,
    bs_ref,
    q_ref,
    k_ref,
    v_ref,
    nk_ref,
    nv_ref,
    keep_ref,
    w_ref,
    readout_ref,
    gain_ref,
    mean_all,
    lse_all,
    flat_ref,
    y_ref,
    order_ref,
    left_ref,
    half_ref,
    far_half,
    sum_ref,
    stat_all,
    local_sem,
    arrive_sem,
    sent_sem,
):
    grp = lax.axis_index("grp")
    mine = lax.axis_index("ctx")
    core = lax.axis_index("head")
    pairs, width = q_ref.shape
    heads = pairs // answer_len
    group = heads // kv_here
    tokens = k_ref.shape[0]
    sources, ablations = keep_ref.shape
    slots = slot_count(ctx_size, pairs)
    lines = flat_ref.shape[0] // pairs * answer_len
    compact = len(left_ref.shape) == 3
    sides, _, wide = w_ref.shape
    half = wide * sides // head_size
    chunk = half_ref.shape[3]
    partner = lax.rem(core + 1, head_size)
    turn = [partner, core]
    theirs, ours = (0, 1) if compact else (partner, core)
    scale = width ** (-0.5)
    rows = ablations * answer_len
    per = LANES // pairs
    devices = ctx_size * head_size

    def flips(position, size):
        return [bit * (1 - 2 * lax.rem(position // bit, 2)) for bit in powers(size)]

    ctx_flips, core_flips = flips(mine, ctx_size), flips(core, head_size)

    def flipped(position, deltas, mask):
        for i, delta in enumerate(deltas):
            if mask >> i & 1:
                position = position + delta
        return position

    def other(mask):
        return (
            grp,
            flipped(mine, ctx_flips, mask // head_size),
            flipped(core, core_flips, mask % head_size),
        )

    barrier = pltpu.get_barrier_semaphore()
    for mask in range(devices - 1, 0, -1):
        pl.semaphore_signal(
            barrier, inc=1, device_id=other(mask), device_id_type=pl.DeviceIdType.MESH
        )

    loads = [
        pltpu.make_async_copy(source, target, local_sem.at[min(max(i, 1), 3) - 1])
        for i, (source, target) in enumerate(
            (
                (q_hbm, q_ref),
                (k_hbm, k_ref),
                (v_hbm, v_ref),
                (nk_hbm, nk_ref),
                (nv_hbm, nv_ref),
                (keep_hbm, keep_ref),
                (bs_hbm, bs_ref),
                (readout_hbm, readout_ref),
                (gain_hbm, gain_ref),
            )
        )
    ]
    for copy in loads:
        copy.start()
    copies_w = [
        pltpu.make_async_copy(
            w_hbm.at[:, pl.ds(pl.multiple_of(turn[j] * half, LANES), half)] if compact else w_hbm,
            w_ref.at[j],
            local_sem.at[3],
        )
        for j in range(sides)
    ]
    for copy in copies_w:
        copy.start()

    loads[0].wait()
    loads[1].wait()
    queries = q_ref[...]
    scores = lax.dot_general(queries, k_ref[...], NT, preferred_element_type=F32) * scale
    near = lax.rem(iota((pairs, tokens), 1), kv_here) == lax.rem(
        iota((pairs, tokens), 0) // group, kv_here
    )
    top = jnp.max(jnp.where(near, scores, LOW), axis=1, keepdims=True)
    expo = jnp.where(near, jnp.exp(scores - top), 0.0)
    total = jnp.sum(expo, axis=1, keepdims=True)
    loads[2].wait()
    summed = jnp.dot(expo.astype(BF16), v_ref[...], preferred_element_type=F32)
    mean = summed / total
    lse = top + jnp.log(total)
    lse_all[mine] = to_row(jnp.concatenate([lse] * per, axis=0))
    pieces = mean_all.shape[0]
    some = heads // pieces
    for piece in range(pieces):
        for t in range(answer_len):
            first = t * heads + piece * some
            mean_all[piece, mine, pl.ds(t * some, some), :] = mean[first : first + some].astype(
                BF16
            )

    pl.semaphore_wait(barrier, devices - 1)

    sent_mean, sent_lse, sent_half, sent_stat = [sent_sem.at[i] for i in range(4)]
    parts = half // chunk
    arrive_mean = [arrive_sem.at[piece] for piece in range(pieces)]
    arrive_half = [arrive_sem.at[pieces + part] for part in range(parts)]
    arrive_stat = arrive_sem.at[pieces + parts]
    arrive_lse = arrive_sem.at[pieces + parts + 1]

    def remote(source, target, send, recv, device):
        return pltpu.make_async_remote_copy(
            src_ref=source,
            dst_ref=target,
            send_sem=send,
            recv_sem=recv,
            device_id=device,
            device_id_type=pl.DeviceIdType.MESH,
        )

    def to_peer(source, send, recv, k):
        place = ctx_size - 1 - k
        peer = jnp.where(place <= mine, place - 1, place)
        remote(source, source, send, recv, (grp, peer, core)).start()

    def bytes_of(block, send, recv):
        return remote(block, block, send, recv, (grp, mine, partner))

    all_lse = bytes_of(lse_all.at[pl.ds(0, ctx_size - 1)], sent_lse, arrive_lse)
    all_mean = [
        bytes_of(mean_all.at[piece, pl.ds(0, ctx_size - 1)], sent_mean, arrive_mean[piece])
        for piece in range(pieces)
    ]

    def send_to(peers, kinds):
        for kind in kinds:
            for k in peers:
                if kind < 0:
                    to_peer(lse_all.at[mine], sent_lse, arrive_lse, k)
                else:
                    to_peer(mean_all.at[kind, mine], sent_mean, arrive_mean[kind], k)

    first = range(1)
    later = range(1, ctx_size - 1)
    send_to(first, range(-1, pieces))
    send_to(later, range(-1, pieces))

    for copy in loads[3:]:
        copy.wait()
    owns = nk_ref.shape[0]
    own_scores = lax.dot_general(queries, nk_ref[...], NT, preferred_element_type=F32) * scale
    place = iota((pairs, owns), 1)
    pair = iota((pairs, owns), 0)
    allowed = (lax.rem(place, kv_here) == lax.rem(pair // group, kv_here)) & (
        place // kv_here <= pair // heads
    )
    own_top = jnp.max(jnp.where(allowed, own_scores, LOW), axis=1, keepdims=True)
    own_expo = jnp.where(allowed, jnp.exp(own_scores - own_top), 0.0)
    own_total = jnp.sum(own_expo, axis=1, keepdims=True)
    own_probs = own_expo.astype(BF16).astype(F32)
    own_values = nv_ref[...].astype(F32)
    own_sum = jnp.zeros((pairs, width), F32)
    for i in range(owns):
        own_sum += own_probs[:, i : i + 1] * own_values[i : i + 1, :]
    flat_ref[pl.ds(ctx_size * pairs, pairs), :] = own_sum / own_total
    for slot in range(ctx_size + 1, flat_ref.shape[0] // pairs):
        flat_ref[pl.ds(slot * pairs, pairs), :] = jnp.zeros((pairs, width), F32)
    own_lse = to_row(jnp.concatenate([own_top + jnp.log(own_total)] * per, axis=0))

    keep = keep_ref[...].astype(F32)
    repeat = (iota((rows, ablations), 0) // answer_len == iota((rows, ablations), 1)).astype(F32)
    keep_rows = lax.dot_general(repeat, keep, NT, preferred_element_type=F32)
    lane = iota((1, LANES), 1)
    part = lane // pairs
    same = lax.rem(iota((rows, LANES), 1), pairs) // heads == lax.rem(
        iota((rows, LANES), 0), answer_len
    )
    masks = []
    for tile in range(slots // per):
        source = jnp.full((1, LANES), -1, jnp.int32)
        own_lane = jnp.zeros((1, LANES), F32)
        for k in range(per):
            slot = tile * per + k
            if slot < ctx_size:
                source = jnp.where(part == k, bs_ref[slot], source)
            if slot == ctx_size:
                own_lane = jnp.where(part == k, 1.0, own_lane)
        chosen = (iota((sources, LANES), 0) == source).astype(F32)
        kept = jnp.dot(keep_rows, chosen, preferred_element_type=F32) + own_lane
        masks.append((kept > 0.5) & same)

    eye = (iota((sources, sources), 0) == iota((sources, sources), 1)).astype(F32)
    keep_cols = lax.dot_general(keep, repeat, NT, preferred_element_type=F32)
    gram = lax.dot_general(keep, keep, NT, preferred_element_type=F32)
    count = jnp.sum(keep, axis=1, keepdims=True)
    count_row = jnp.sum(keep_rows, axis=0, keepdims=True) / answer_len
    system = gram - count * count_row / ablations + RIDGE * eye
    centered = keep_cols - count / ablations

    def sweep(k, state):
        on_row = iota((sources, sources), 0) == k
        on_col = iota((sources, sources), 1) == k
        row = jnp.sum(jnp.where(on_row, state, 0.0), axis=0, keepdims=True)
        col = jnp.sum(jnp.where(on_col, state, 0.0), axis=1, keepdims=True)
        pivot = jnp.sum(jnp.where(on_col[0:1], row, 0.0), axis=1, keepdims=True)
        inverse = 1.0 / pivot
        return jnp.where(
            on_row,
            jnp.where(on_col, -inverse, row * inverse),
            jnp.where(on_col, col * inverse, state - col * (row * inverse)),
        )

    swept = lax.fori_loop(0, sources, sweep, system, unroll=sources <= 8)
    solver_ref[...] = -jnp.dot(swept, centered, precision=lax.Precision.HIGHEST, preferred_element_type=F32)

    if compact:
        spot = iota((1, heads * lines), 1)
        line = lax.rem(spot, lines)
        wanted = (
            line // answer_len * pairs + lax.rem(line, answer_len) * heads + spot // lines
        )
        order_ref[...] = (iota(order_ref.shape, 0) == wanted).astype(BF16)
    all_lse.wait_recv()

    def make_coef():
        tops = []
        for tile in range(slots // per):
            line = jnp.full((1, LANES), LOW, F32)
            for k in range(per):
                slot = tile * per + k
                if slot <= ctx_size:
                    here = lse_all[slot] if slot < ctx_size else own_lse
                    line = jnp.where(part == k, here, line)
            tops.append(jnp.where(masks[tile], line, LOW))

        def across(value, op):
            shift = pairs
            while shift < LANES:
                value = op(value, pltpu.roll(value, shift, 1))
                shift *= 2
            return value

        overall = across(functools.reduce(jnp.maximum, tops), jnp.maximum)
        weights = [jnp.where(m, jnp.exp(s - overall), 0.0) for m, s in zip(masks, tops)]
        denom = across(functools.reduce(jnp.add, weights), jnp.add)
        inverse = 1.0 / jnp.where(same, denom, 1.0)
        coef = jnp.concatenate([(w * inverse).astype(BF16) for w in weights], axis=1)

        return coef

    def arrange(coef):
        if compact:
            coef = jnp.dot(coef, order_ref[...], preferred_element_type=F32).astype(BF16)
        return coef

    pair_up = 2

    def lines_of(k):
        return flat_ref[pl.ds(k, lines, stride=heads), :].astype(BF16)

    def project(j, h):
        outs = []
        for k in range(h, h + pair_up):
            left = (
                left_ref[h // pair_up, pl.ds((k - h) * lines, lines), :] if compact else lines_of(k)
            )
            outs.append(
                jnp.dot(
                    left, w_ref[j, pl.ds(k * width, width), :], preferred_element_type=F32
                )
            )
        if compact:
            y_ref[j, pl.ds(h * lines, pair_up * lines), :] = jnp.concatenate(
                outs, axis=0
            ).astype(BF16)
        else:
            for k in range(pair_up):
                for c in range(wide // LANES):
                    y_ref[c, pl.ds(h + k, lines, stride=heads), :] = outs[k][
                        :, c * LANES : (c + 1) * LANES
                    ]

    def mix(j, part):
        if compact:
            right = y_ref[j, :, pl.ds(part * chunk, chunk)]
        else:
            right = jnp.concatenate(
                [y_ref[c].astype(BF16) for c in range(wide // LANES)], axis=1
            )[:, j * half : (j + 1) * half]
        half_ref[j, part] = jnp.dot(coef, right, preferred_element_type=F32)

    for copy in copies_w:
        copy.wait()
    natural = make_coef()
    swaps = []
    for piece in range(pieces):
        all_mean[piece].wait_recv()
        for slot in range(ctx_size):
            for t in range(answer_len):
                flat_ref[pl.ds(slot * pairs + t * heads + piece * some, some), :] = mean_all[
                    piece, slot, pl.ds(t * some, some), :
                ].astype(F32)
        here = range(piece * some, (piece + 1) * some, pair_up)
        if piece == 0:
            coef = arrange(natural)
        for h in here:
            if compact:
                left_ref[h // pair_up] = jnp.concatenate(
                    [lines_of(k) for k in range(h, h + pair_up)], axis=0
                )
            project(0, h)
    for part in range(half // chunk):
        for j in range(1 if compact else head_size):
            mix(j, part)
        copy = remote(
            half_ref.at[theirs, part],
            far_half.at[part],
            sent_half,
            arrive_half[part],
            (grp, mine, partner),
        )
        copy.start()
        swaps.append(copy)
    if compact:
        for h in range(0, heads, pair_up):
            project(1, h)
        for part in range(half // chunk):
            mix(1, part)
    row_token = lax.rem(iota((rows, chunk), 0), answer_len)
    squared, read = 0.0, 0.0
    for part, copy in enumerate(swaps):
        here = pl.ds(part * chunk, chunk)
        reader = [
            readout_ref[t : t + 1, here].astype(F32) * gain_ref[:, here]
            for t in range(answer_len)
        ]
        reading = jnp.broadcast_to(reader[0], (rows, chunk))
        for t in range(1, answer_len):
            reading = jnp.where(row_token == t, reader[t], reading)
        copy.wait_recv()
        block = (half_ref[ours, part] + far_half[part]).astype(BF16)
        feature = block.astype(F32)
        sum_ref[part] = block
        squared += fold(feature * feature)
        read += fold(feature * reading)
    squares, dotted = row_sums(squared), row_sums(read)
    me = mine * head_size + core
    stat_all[me] = jnp.concatenate([squares, dotted], axis=0)
    for mask in range(devices - 1, 0, -1):
        remote(stat_all.at[me], stat_all.at[me], sent_stat, arrive_stat, other(mask)).start()
    all_stat = bytes_of(stat_all.at[pl.ds(0, devices - 1)], sent_stat, arrive_stat)
    all_lse.wait_send()
    for part in range(parts):
        proj_ref[:, :, pl.ds(part * chunk, chunk)] = (
            sum_ref[part].astype(F32).reshape(ablations, answer_len, chunk).astype(BF16)
        )
    all_stat.wait_recv()
    summary = stat_all[0]
    for i in range(1, devices):
        summary = summary + stat_all[i]
    summary_ref[...] = summary
    for copy in (
        bytes_of(mean_all.at[:, pl.ds(0, ctx_size - 1)], sent_mean, arrive_lse),
        bytes_of(far_half, sent_half, arrive_lse),
        all_stat,
    ):
        copy.wait_send()


def finish(
    answer_len,
    features,
    proj_ref,
    summary_ref,
    solver_ref,
    proj_out,
    logit_out,
    attr_out,
    logit_ref,
    attr_ref,
    sem,
):
    ablations = proj_ref.shape[0]
    sources = solver_ref.shape[0]
    rows = ablations * answer_len
    stores = [pltpu.make_async_copy(proj_ref, proj_out, sem.at[0])]
    stores[0].start()
    summary, solver = summary_ref[...], solver_ref[...]
    logits = summary[1:2] * lax.rsqrt(summary[0:1] / features + EPSILON)
    spread = jnp.transpose(jnp.broadcast_to(logits, (LANES, LANES)))
    picked = jnp.where(
        iota((rows, ablations), 0) // answer_len == iota((rows, ablations), 1),
        spread[:, :ablations],
        0.0,
    )
    row_of = lax.rem(iota((rows, ablations), 0), answer_len)
    for t in range(answer_len):
        logit_ref[t : t + 1, :] = jnp.sum(
            jnp.where(row_of == t, picked, 0.0), axis=0, keepdims=True
        )
    target_dev = logits - jnp.sum(logits, axis=1, keepdims=True) / rows
    answer = jnp.sum(solver * target_dev, axis=1, keepdims=True)
    diagonal = iota((sources, sources), 0) == iota((sources, sources), 1)
    attr_ref[...] = jnp.sum(jnp.where(diagonal, answer, 0.0), axis=0, keepdims=True)
    stores.append(pltpu.make_async_copy(logit_ref, logit_out, sem.at[0]))
    stores.append(pltpu.make_async_copy(attr_ref, attr_out, sem.at[0]))
    for copy in stores[1:]:
        copy.start()
    for copy in stores:
        copy.wait()


def on_device(
    ctx_size,
    head_size,
    queries,
    keys,
    values,
    new_keys,
    new_values,
    keep,
    block_source,
    out_weight,
    readout,
    gain,
):
    answer_len, heads, width = queries.shape
    tokens, kv_here, _ = keys.shape
    assert tokens == BLOCK
    pairs = answer_len * heads
    ablations, sources = keep.shape
    rows = ablations * answer_len
    depth, columns = out_weight.shape
    half = columns // head_size
    per = LANES // pairs
    assert rows == LANES and per * pairs == LANES and width == LANES
    slots = slot_count(ctx_size, pairs)
    lines = -(-slots * answer_len // 8) * 8
    compact = lines <= 32 and half % LANES == 0
    if not compact:
        lines = slots * answer_len
    devices = ctx_size * head_size
    pieces = 2
    sides = head_size if compact else 1
    chunk = half
    parts = half // chunk
    assert head_size == 2
    assert all(size & (size - 1) == 0 for size in (ctx_size, head_size))
    hbm = pl.BlockSpec(memory_space=pltpu.HBM)
    vmem = pl.BlockSpec(memory_space=pltpu.VMEM)
    projected, summary, solver = pl.pallas_call(
        functools.partial(kernel, ctx_size, head_size, answer_len, kv_here),
        out_shape=(
            jax.ShapeDtypeStruct((ablations, answer_len, half), BF16),
            jax.ShapeDtypeStruct((2, rows), F32),
            jax.ShapeDtypeStruct((sources, rows), F32),
        ),
        in_specs=[hbm] * 10,
        out_specs=(vmem, vmem, vmem),
        scratch_shapes=[
            pltpu.SMEM((ctx_size,), jnp.int32),
            pltpu.VMEM((pairs, width), BF16),
            pltpu.VMEM((tokens * kv_here, width), BF16),
            pltpu.VMEM((tokens * kv_here, width), BF16),
            pltpu.VMEM((answer_len * kv_here, width), BF16),
            pltpu.VMEM((answer_len * kv_here, width), BF16),
            pltpu.VMEM((sources, ablations), jnp.int32),
            pltpu.VMEM((sides, depth, columns // sides), BF16),
            pltpu.VMEM((answer_len, half), BF16),
            pltpu.VMEM((1, half), F32),
            pltpu.VMEM((pieces, ctx_size, pairs // pieces, width), BF16),
            pltpu.VMEM((ctx_size, 1, LANES), F32),
            pltpu.VMEM((heads * lines, width), F32),
            pltpu.VMEM((head_size, heads * lines, half), BF16)
            if compact
            else pltpu.VMEM((columns // LANES, heads * lines, LANES), F32),
            pltpu.VMEM((slots * pairs, heads * lines) if compact else (8, LANES), BF16),
            pltpu.VMEM((heads // 2, 2 * lines, width) if compact else (16, LANES), BF16),
            pltpu.VMEM((head_size, parts, rows, chunk), F32),
            pltpu.VMEM((parts, rows, chunk), F32),
            pltpu.VMEM((parts, rows, chunk), BF16),
            pltpu.VMEM((devices, 2, LANES), F32),
            pltpu.SemaphoreType.DMA((4,)),
            pltpu.SemaphoreType.DMA((pieces + parts + 2,)),
            pltpu.SemaphoreType.DMA((4,)),
        ],
        compiler_params=pltpu.CompilerParams(
            collective_id=0, has_side_effects=True, vmem_limit_bytes=48 << 20
        ),
        name="attribute",
    )(
        *(pltpu.with_memory_space_constraint(x, pltpu.HBM) for x in (
        block_source,
        queries.reshape(pairs, width),
        keys.reshape(tokens * kv_here, width),
        values.reshape(tokens * kv_here, width),
        new_keys.reshape(-1, width),
        new_values.reshape(-1, width),
        keep.T,
        out_weight,
        readout,
        gain.reshape(1, -1),
        )),
    )
    projected, logits, attribution = pl.pallas_call(
        functools.partial(finish, answer_len, columns * ctx_size),
        out_shape=(
            jax.ShapeDtypeStruct(projected.shape, BF16),
            jax.ShapeDtypeStruct((answer_len, ablations), F32),
            jax.ShapeDtypeStruct((1, sources), F32),
        ),
        in_specs=[vmem] * 3,
        compiler_params=pltpu.CompilerParams(vmem_limit_bytes=2 << 20),
        out_specs=[hbm] * 3,
        scratch_shapes=[
            pltpu.VMEM((answer_len, ablations), F32),
            pltpu.VMEM((1, sources), F32),
            pltpu.SemaphoreType.DMA((1,)),
        ],
        name="finish",
    )(projected, summary, solver)
    return projected, logits.T, attribution.reshape(sources)


def solution(mesh):
    in_specs = (
        P("grp", "head", None),
        P(("grp", "ctx"), "head", None),
        P(("grp", "ctx"), "head", None),
        P("grp", "head", None),
        P("grp", "head", None),
        P("grp", None),
        P("grp"),
        P("head", "ctx"),
        P("grp", ("ctx", "head")),
        P(("ctx", "head")),
    )
    out_specs = (P("grp", None, ("ctx", "head")), P("grp", None), P("grp"))
    return jax.shard_map(
        functools.partial(on_device, mesh.shape["ctx"], mesh.shape["head"]),
        mesh=mesh,
        in_specs=in_specs,
        out_specs=out_specs,
        check_vma=False,
    )
```

```python
import functools

import jax
import jax.numpy as jnp
from jax import lax
from jax.experimental import pallas as pl
from jax.experimental.pallas import tpu as pltpu
from jax.sharding import PartitionSpec as P

BLOCK = 512
EPSILON = 1e-05
RIDGE = 1.0
LOW = -1e30
LANES = 128
F32 = jnp.float32
BF16 = jnp.bfloat16
NT = (((1,), (1,)), ((), ()))


def iota(shape, axis):
    return lax.broadcasted_iota(jnp.int32, shape, axis)


def powers(size):
    return [1 << i for i in range(size.bit_length() - 1)]


def slot_count(ctx_size, pairs):
    per = LANES // pairs
    return -(-(ctx_size + 1) // per) * per


def to_row(column):
    return jnp.transpose(jnp.broadcast_to(column, (LANES, LANES)))[0:1, :]


def fold(block):
    step = min(block.shape[1], LANES)
    return sum(block[:, i : i + step] for i in range(0, block.shape[1], step))


def row_sums(block):
    if block.shape[1] < LANES:
        return to_row(jnp.sum(block, axis=1, keepdims=True))
    return jnp.sum(jnp.transpose(block), axis=0, keepdims=True)


def kernel(
    ctx_size,
    head_size,
    answer_len,
    kv_here,
    bs_hbm,
    q_hbm,
    k_hbm,
    v_hbm,
    nk_hbm,
    nv_hbm,
    keep_hbm,
    w_hbm,
    readout_hbm,
    gain_hbm,
    proj_ref,
    summary_ref,
    solver_ref,
    bs_ref,
    q_ref,
    k_ref,
    v_ref,
    nk_ref,
    nv_ref,
    keep_ref,
    w_ref,
    readout_ref,
    gain_ref,
    mean_all,
    lse_all,
    flat_ref,
    y_ref,
    order_ref,
    left_ref,
    half_ref,
    give_ref,
    far_half,
    sum_ref,
    stat_all,
    local_sem,
    arrive_sem,
    sent_sem,
):
    grp = lax.axis_index("grp")
    mine = lax.axis_index("ctx")
    core = lax.axis_index("head")
    pairs, width = q_ref.shape
    heads = pairs // answer_len
    group = heads // kv_here
    tokens = k_ref.shape[0]
    sources, ablations = keep_ref.shape
    slots = slot_count(ctx_size, pairs)
    lines = flat_ref.shape[0] // pairs * answer_len
    compact = len(left_ref.shape) == 3
    sides, _, wide = w_ref.shape
    half = wide * sides // head_size
    chunk = half_ref.shape[3]
    partner = lax.rem(core + 1, head_size)
    turn = [partner, core]
    theirs, ours = (0, 1) if compact else (partner, core)
    scale = width ** (-0.5)
    rows = ablations * answer_len
    per = LANES // pairs
    devices = ctx_size * head_size

    def flips(position, size):
        return [bit * (1 - 2 * lax.rem(position // bit, 2)) for bit in powers(size)]

    ctx_flips, core_flips = flips(mine, ctx_size), flips(core, head_size)

    def flipped(position, deltas, mask):
        for i, delta in enumerate(deltas):
            if mask >> i & 1:
                position = position + delta
        return position

    def other(mask):
        return (
            grp,
            flipped(mine, ctx_flips, mask // head_size),
            flipped(core, core_flips, mask % head_size),
        )

    barrier = pltpu.get_barrier_semaphore()
    for mask in range(devices - 1, 0, -1):
        pl.semaphore_signal(
            barrier, inc=1, device_id=other(mask), device_id_type=pl.DeviceIdType.MESH
        )

    loads = [
        pltpu.make_async_copy(source, target, local_sem.at[min(max(i, 1), 3) - 1])
        for i, (source, target) in enumerate(
            (
                (q_hbm, q_ref),
                (k_hbm, k_ref),
                (v_hbm, v_ref),
                (nk_hbm, nk_ref),
                (nv_hbm, nv_ref),
                (keep_hbm, keep_ref),
                (bs_hbm, bs_ref),
                (readout_hbm, readout_ref),
                (gain_hbm, gain_ref),
            )
        )
    ]
    for copy in loads:
        copy.start()
    copies_w = [
        pltpu.make_async_copy(
            w_hbm.at[:, pl.ds(pl.multiple_of(turn[j] * half, LANES), half)] if compact else w_hbm,
            w_ref.at[j],
            local_sem.at[3],
        )
        for j in range(sides)
    ]
    for copy in copies_w:
        copy.start()

    loads[0].wait()
    loads[1].wait()
    queries = q_ref[...]
    scores = lax.dot_general(queries, k_ref[...], NT, preferred_element_type=F32) * scale
    near = lax.rem(iota((pairs, tokens), 1), kv_here) == lax.rem(
        iota((pairs, tokens), 0) // group, kv_here
    )
    top = jnp.max(jnp.where(near, scores, LOW), axis=1, keepdims=True)
    expo = jnp.where(near, jnp.exp(scores - top), 0.0)
    total = jnp.sum(expo, axis=1, keepdims=True)
    loads[2].wait()
    summed = jnp.dot(expo.astype(BF16), v_ref[...], preferred_element_type=F32)
    mean = summed / total
    lse = top + jnp.log(total)
    lse_all[mine] = to_row(jnp.concatenate([lse] * per, axis=0))
    pieces = mean_all.shape[0]
    some = heads // pieces
    for piece in range(pieces):
        for t in range(answer_len):
            first = t * heads + piece * some
            mean_all[piece, mine, pl.ds(t * some, some), :] = mean[first : first + some].astype(
                BF16
            )

    pl.semaphore_wait(barrier, devices - 1)

    sent_mean, sent_lse, sent_half, sent_stat = [sent_sem.at[i] for i in range(4)]
    parts = half // chunk
    arrive_mean = [arrive_sem.at[piece] for piece in range(pieces)]
    arrive_half = [arrive_sem.at[pieces + part] for part in range(parts)]
    arrive_stat = arrive_sem.at[pieces + parts]
    arrive_lse = arrive_sem.at[pieces + parts + 1]

    def remote(source, target, send, recv, device):
        return pltpu.make_async_remote_copy(
            src_ref=source,
            dst_ref=target,
            send_sem=send,
            recv_sem=recv,
            device_id=device,
            device_id_type=pl.DeviceIdType.MESH,
        )

    def to_peer(source, send, recv, k):
        place = ctx_size - 1 - k
        peer = jnp.where(place <= mine, place - 1, place)
        remote(source, source, send, recv, (grp, peer, core)).start()

    def bytes_of(block, send, recv):
        return remote(block, block, send, recv, (grp, mine, partner))

    all_lse = bytes_of(lse_all.at[pl.ds(0, ctx_size - 1)], sent_lse, arrive_lse)
    all_mean = [
        bytes_of(mean_all.at[piece, pl.ds(0, ctx_size - 1)], sent_mean, arrive_mean[piece])
        for piece in range(pieces)
    ]

    def send_to(peers, kinds):
        for kind in kinds:
            for k in peers:
                if kind < 0:
                    to_peer(lse_all.at[mine], sent_lse, arrive_lse, k)
                else:
                    to_peer(mean_all.at[kind, mine], sent_mean, arrive_mean[kind], k)

    first = range(1)
    later = range(ctx_size - 2, 0, -1)
    send_to(first, range(-1, pieces))
    send_to(later, range(-1, pieces))

    for copy in loads[3:]:
        copy.wait()
    owns = nk_ref.shape[0]
    own_scores = lax.dot_general(queries, nk_ref[...], NT, preferred_element_type=F32) * scale
    place = iota((pairs, owns), 1)
    pair = iota((pairs, owns), 0)
    allowed = (lax.rem(place, kv_here) == lax.rem(pair // group, kv_here)) & (
        place // kv_here <= pair // heads
    )
    own_top = jnp.max(jnp.where(allowed, own_scores, LOW), axis=1, keepdims=True)
    own_expo = jnp.where(allowed, jnp.exp(own_scores - own_top), 0.0)
    own_total = jnp.sum(own_expo, axis=1, keepdims=True)
    own_probs = own_expo.astype(BF16).astype(F32)
    own_values = nv_ref[...].astype(F32)
    own_sum = jnp.zeros((pairs, width), F32)
    for i in range(owns):
        own_sum += own_probs[:, i : i + 1] * own_values[i : i + 1, :]
    flat_ref[pl.ds(ctx_size * pairs, pairs), :] = own_sum / own_total
    for slot in range(ctx_size + 1, flat_ref.shape[0] // pairs):
        flat_ref[pl.ds(slot * pairs, pairs), :] = jnp.zeros((pairs, width), F32)
    own_lse = to_row(jnp.concatenate([own_top + jnp.log(own_total)] * per, axis=0))

    keep = keep_ref[...].astype(F32)
    repeat = (iota((rows, ablations), 0) // answer_len == iota((rows, ablations), 1)).astype(F32)
    keep_rows = lax.dot_general(repeat, keep, NT, preferred_element_type=F32)
    lane = iota((1, LANES), 1)
    part = lane // pairs
    same = lax.rem(iota((rows, LANES), 1), pairs) // heads == lax.rem(
        iota((rows, LANES), 0), answer_len
    )
    masks = []
    for tile in range(slots // per):
        source = jnp.full((1, LANES), -1, jnp.int32)
        own_lane = jnp.zeros((1, LANES), F32)
        for k in range(per):
            slot = tile * per + k
            if slot < ctx_size:
                source = jnp.where(part == k, bs_ref[slot], source)
            if slot == ctx_size:
                own_lane = jnp.where(part == k, 1.0, own_lane)
        chosen = (iota((sources, LANES), 0) == source).astype(F32)
        kept = jnp.dot(keep_rows, chosen, preferred_element_type=F32) + own_lane
        masks.append((kept > 0.5) & same)

    eye = (iota((sources, sources), 0) == iota((sources, sources), 1)).astype(F32)
    keep_cols = lax.dot_general(keep, repeat, NT, preferred_element_type=F32)
    gram = lax.dot_general(keep, keep, NT, preferred_element_type=F32)
    count = jnp.sum(keep, axis=1, keepdims=True)
    count_row = jnp.sum(keep_rows, axis=0, keepdims=True) / answer_len
    system = gram - count * count_row / ablations + RIDGE * eye
    centered = keep_cols - count / ablations

    def sweep(k, state):
        on_row = iota((sources, sources), 0) == k
        on_col = iota((sources, sources), 1) == k
        row = jnp.sum(jnp.where(on_row, state, 0.0), axis=0, keepdims=True)
        col = jnp.sum(jnp.where(on_col, state, 0.0), axis=1, keepdims=True)
        pivot = jnp.sum(jnp.where(on_col[0:1], row, 0.0), axis=1, keepdims=True)
        inverse = 1.0 / pivot
        return jnp.where(
            on_row,
            jnp.where(on_col, -inverse, row * inverse),
            jnp.where(on_col, col * inverse, state - col * (row * inverse)),
        )

    swept = lax.fori_loop(0, sources, sweep, system, unroll=sources <= 8)
    solver_ref[...] = -jnp.dot(swept, centered, precision=lax.Precision.HIGHEST, preferred_element_type=F32)

    if compact:
        spot = iota((1, heads * lines), 1)
        line = lax.rem(spot, lines)
        wanted = (
            line // answer_len * pairs + lax.rem(line, answer_len) * heads + spot // lines
        )
        order_ref[...] = (iota(order_ref.shape, 0) == wanted).astype(BF16)
    all_lse.wait_recv()

    def make_coef():
        tops = []
        for tile in range(slots // per):
            line = jnp.full((1, LANES), LOW, F32)
            for k in range(per):
                slot = tile * per + k
                if slot <= ctx_size:
                    here = lse_all[slot] if slot < ctx_size else own_lse
                    line = jnp.where(part == k, here, line)
            tops.append(jnp.where(masks[tile], line, LOW))

        def across(value, op):
            shift = pairs
            while shift < LANES:
                value = op(value, pltpu.roll(value, shift, 1))
                shift *= 2
            return value

        overall = across(functools.reduce(jnp.maximum, tops), jnp.maximum)
        weights = [jnp.where(m, jnp.exp(s - overall), 0.0) for m, s in zip(masks, tops)]
        denom = across(functools.reduce(jnp.add, weights), jnp.add)
        inverse = 1.0 / jnp.where(same, denom, 1.0)
        coef = jnp.concatenate([(w * inverse).astype(BF16) for w in weights], axis=1)

        return coef

    def arrange(coef):
        if compact:
            coef = jnp.dot(coef, order_ref[...], preferred_element_type=F32).astype(BF16)
        return coef

    pair_up = 2

    def lines_of(k):
        return flat_ref[pl.ds(k, lines, stride=heads), :].astype(BF16)

    def project(j, h):
        outs = []
        for k in range(h, h + pair_up):
            left = (
                left_ref[h // pair_up, pl.ds((k - h) * lines, lines), :] if compact else lines_of(k)
            )
            outs.append(
                jnp.dot(
                    left, w_ref[j, pl.ds(k * width, width), :], preferred_element_type=F32
                )
            )
        if compact:
            y_ref[j, pl.ds(h * lines, pair_up * lines), :] = jnp.concatenate(
                outs, axis=0
            ).astype(BF16)
        else:
            for k in range(pair_up):
                for c in range(wide // LANES):
                    y_ref[c, pl.ds(h + k, lines, stride=heads), :] = outs[k][
                        :, c * LANES : (c + 1) * LANES
                    ]

    def mix(j, part):
        if compact:
            right = y_ref[j, :, pl.ds(part * chunk, chunk)]
        else:
            right = jnp.concatenate(
                [y_ref[c].astype(BF16) for c in range(wide // LANES)], axis=1
            )[:, j * half : (j + 1) * half]
        half_ref[j, part] = jnp.dot(coef, right, preferred_element_type=F32)

    for copy in copies_w:
        copy.wait()
    natural = make_coef()
    swaps = []
    for piece in range(pieces):
        all_mean[piece].wait_recv()
        for slot in range(ctx_size):
            for t in range(answer_len):
                flat_ref[pl.ds(slot * pairs + t * heads + piece * some, some), :] = mean_all[
                    piece, slot, pl.ds(t * some, some), :
                ].astype(F32)
        here = range(piece * some, (piece + 1) * some, pair_up)
        if piece == 0:
            coef = arrange(natural)
        for h in here:
            if compact:
                left_ref[h // pair_up] = jnp.concatenate(
                    [lines_of(k) for k in range(h, h + pair_up)], axis=0
                )
            project(0, h)
    for part in range(half // chunk):
        for j in range(1 if compact else head_size):
            mix(j, part)
        give_ref[part] = half_ref[theirs, part].astype(BF16)
        copy = remote(
            give_ref.at[part],
            far_half.at[part],
            sent_half,
            arrive_half[part],
            (grp, mine, partner),
        )
        copy.start()
        swaps.append(copy)
    if compact:
        for h in range(0, heads, pair_up):
            project(1, h)
        for part in range(half // chunk):
            mix(1, part)
    row_token = lax.rem(iota((rows, chunk), 0), answer_len)
    squared, read = 0.0, 0.0
    for part, copy in enumerate(swaps):
        here = pl.ds(part * chunk, chunk)
        reader = [
            readout_ref[t : t + 1, here].astype(F32) * gain_ref[:, here]
            for t in range(answer_len)
        ]
        reading = jnp.broadcast_to(reader[0], (rows, chunk))
        for t in range(1, answer_len):
            reading = jnp.where(row_token == t, reader[t], reading)
        copy.wait_recv()
        block = (half_ref[ours, part] + far_half[part].astype(F32)).astype(BF16)
        feature = block.astype(F32)
        sum_ref[part] = block
        squared += fold(feature * feature)
        read += fold(feature * reading)
    squares, dotted = row_sums(squared), row_sums(read)
    me = mine * head_size + core
    stat_all[me] = jnp.concatenate([squares, dotted], axis=0)
    for mask in range(devices - 1, 0, -1):
        remote(stat_all.at[me], stat_all.at[me], sent_stat, arrive_stat, other(mask)).start()
    all_stat = bytes_of(stat_all.at[pl.ds(0, devices - 1)], sent_stat, arrive_stat)
    all_lse.wait_send()
    for part in range(parts):
        proj_ref[:, :, pl.ds(part * chunk, chunk)] = (
            sum_ref[part].astype(F32).reshape(ablations, answer_len, chunk).astype(BF16)
        )
    all_stat.wait_recv()
    summary = stat_all[0]
    for i in range(1, devices):
        summary = summary + stat_all[i]
    summary_ref[...] = summary
    for copy in (
        bytes_of(mean_all.at[:, pl.ds(0, ctx_size - 1)], sent_mean, arrive_lse),
        bytes_of(far_half, sent_half, arrive_lse),
        all_stat,
    ):
        copy.wait_send()


def finish(
    answer_len,
    features,
    proj_ref,
    summary_ref,
    solver_ref,
    proj_out,
    logit_out,
    attr_out,
    logit_ref,
    attr_ref,
    sem,
):
    ablations = proj_ref.shape[0]
    sources = solver_ref.shape[0]
    rows = ablations * answer_len
    stores = [pltpu.make_async_copy(proj_ref, proj_out, sem.at[0])]
    stores[0].start()
    summary, solver = summary_ref[...], solver_ref[...]
    logits = summary[1:2] * lax.rsqrt(summary[0:1] / features + EPSILON)
    spread = jnp.transpose(jnp.broadcast_to(logits, (LANES, LANES)))
    picked = jnp.where(
        iota((rows, ablations), 0) // answer_len == iota((rows, ablations), 1),
        spread[:, :ablations],
        0.0,
    )
    row_of = lax.rem(iota((rows, ablations), 0), answer_len)
    for t in range(answer_len):
        logit_ref[t : t + 1, :] = jnp.sum(
            jnp.where(row_of == t, picked, 0.0), axis=0, keepdims=True
        )
    target_dev = logits - jnp.sum(logits, axis=1, keepdims=True) / rows
    answer = jnp.sum(solver * target_dev, axis=1, keepdims=True)
    diagonal = iota((sources, sources), 0) == iota((sources, sources), 1)
    attr_ref[...] = jnp.sum(jnp.where(diagonal, answer, 0.0), axis=0, keepdims=True)
    stores.append(pltpu.make_async_copy(logit_ref, logit_out, sem.at[0]))
    stores.append(pltpu.make_async_copy(attr_ref, attr_out, sem.at[0]))
    for copy in stores[1:]:
        copy.start()
    for copy in stores:
        copy.wait()


def on_device(
    ctx_size,
    head_size,
    queries,
    keys,
    values,
    new_keys,
    new_values,
    keep,
    block_source,
    out_weight,
    readout,
    gain,
):
    answer_len, heads, width = queries.shape
    tokens, kv_here, _ = keys.shape
    assert tokens == BLOCK
    pairs = answer_len * heads
    ablations, sources = keep.shape
    rows = ablations * answer_len
    depth, columns = out_weight.shape
    half = columns // head_size
    per = LANES // pairs
    assert rows == LANES and per * pairs == LANES and width == LANES
    slots = slot_count(ctx_size, pairs)
    lines = -(-slots * answer_len // 8) * 8
    compact = lines <= 32 and half % LANES == 0
    if not compact:
        lines = slots * answer_len
    devices = ctx_size * head_size
    pieces = 2
    sides = head_size if compact else 1
    chunk = half
    parts = half // chunk
    assert head_size == 2
    assert all(size & (size - 1) == 0 for size in (ctx_size, head_size))
    hbm = pl.BlockSpec(memory_space=pltpu.HBM)
    vmem = pl.BlockSpec(memory_space=pltpu.VMEM)
    projected, summary, solver = pl.pallas_call(
        functools.partial(kernel, ctx_size, head_size, answer_len, kv_here),
        out_shape=(
            jax.ShapeDtypeStruct((ablations, answer_len, half), BF16),
            jax.ShapeDtypeStruct((2, rows), F32),
            jax.ShapeDtypeStruct((sources, rows), F32),
        ),
        in_specs=[hbm] * 10,
        out_specs=(vmem, vmem, vmem),
        scratch_shapes=[
            pltpu.SMEM((ctx_size,), jnp.int32),
            pltpu.VMEM((pairs, width), BF16),
            pltpu.VMEM((tokens * kv_here, width), BF16),
            pltpu.VMEM((tokens * kv_here, width), BF16),
            pltpu.VMEM((answer_len * kv_here, width), BF16),
            pltpu.VMEM((answer_len * kv_here, width), BF16),
            pltpu.VMEM((sources, ablations), jnp.int32),
            pltpu.VMEM((sides, depth, columns // sides), BF16),
            pltpu.VMEM((answer_len, half), BF16),
            pltpu.VMEM((1, half), F32),
            pltpu.VMEM((pieces, ctx_size, pairs // pieces, width), BF16),
            pltpu.VMEM((ctx_size, 1, LANES), F32),
            pltpu.VMEM((heads * lines, width), F32),
            pltpu.VMEM((head_size, heads * lines, half), BF16)
            if compact
            else pltpu.VMEM((columns // LANES, heads * lines, LANES), F32),
            pltpu.VMEM((slots * pairs, heads * lines) if compact else (8, LANES), BF16),
            pltpu.VMEM((heads // 2, 2 * lines, width) if compact else (16, LANES), BF16),
            pltpu.VMEM((head_size, parts, rows, chunk), F32),
            pltpu.VMEM((parts, rows, chunk), BF16),
            pltpu.VMEM((parts, rows, chunk), BF16),
            pltpu.VMEM((parts, rows, chunk), BF16),
            pltpu.VMEM((devices, 2, LANES), F32),
            pltpu.SemaphoreType.DMA((4,)),
            pltpu.SemaphoreType.DMA((pieces + parts + 2,)),
            pltpu.SemaphoreType.DMA((4,)),
        ],
        compiler_params=pltpu.CompilerParams(
            collective_id=0, has_side_effects=True, vmem_limit_bytes=48 << 20
        ),
        name="attribute",
    )(
        *(pltpu.with_memory_space_constraint(x, pltpu.HBM) for x in (
        block_source,
        queries.reshape(pairs, width),
        keys.reshape(tokens * kv_here, width),
        values.reshape(tokens * kv_here, width),
        new_keys.reshape(-1, width),
        new_values.reshape(-1, width),
        keep.T,
        out_weight,
        readout,
        gain.reshape(1, -1),
        )),
    )
    projected, logits, attribution = pl.pallas_call(
        functools.partial(finish, answer_len, columns * ctx_size),
        out_shape=(
            jax.ShapeDtypeStruct(projected.shape, BF16),
            jax.ShapeDtypeStruct((answer_len, ablations), F32),
            jax.ShapeDtypeStruct((1, sources), F32),
        ),
        in_specs=[vmem] * 3,
        compiler_params=pltpu.CompilerParams(vmem_limit_bytes=2 << 20),
        out_specs=[hbm] * 3,
        scratch_shapes=[
            pltpu.VMEM((answer_len, ablations), F32),
            pltpu.VMEM((1, sources), F32),
            pltpu.SemaphoreType.DMA((1,)),
        ],
        name="finish",
    )(projected, summary, solver)
    return projected, logits.T, attribution.reshape(sources)


def solution(mesh):
    in_specs = (
        P("grp", "head", None),
        P(("grp", "ctx"), "head", None),
        P(("grp", "ctx"), "head", None),
        P("grp", "head", None),
        P("grp", "head", None),
        P("grp", None),
        P("grp"),
        P("head", "ctx"),
        P("grp", ("ctx", "head")),
        P(("ctx", "head")),
    )
    out_specs = (P("grp", None, ("ctx", "head")), P("grp", None), P("grp"))
    return jax.shard_map(
        functools.partial(on_device, mesh.shape["ctx"], mesh.shape["head"]),
        mesh=mesh,
        in_specs=in_specs,
        out_specs=out_specs,
        check_vma=False,
    )
```

```python
import functools

import jax
import jax.numpy as jnp
from jax import lax
from jax.experimental import pallas as pl
from jax.experimental.pallas import tpu as pltpu
from jax.sharding import PartitionSpec as P

BLOCK = 512
EPSILON = 1e-05
RIDGE = 1.0
LOW = -1e30
LANES = 128
F32 = jnp.float32
BF16 = jnp.bfloat16
NT = (((1,), (1,)), ((), ()))


def iota(shape, axis):
    return lax.broadcasted_iota(jnp.int32, shape, axis)


def powers(size):
    return [1 << i for i in range(size.bit_length() - 1)]


def slot_count(ctx_size, pairs):
    per = LANES // pairs
    return -(-(ctx_size + 1) // per) * per


def to_row(column):
    return jnp.transpose(jnp.broadcast_to(column, (LANES, LANES)))[0:1, :]


def fold(block):
    step = min(block.shape[1], LANES)
    return sum(block[:, i : i + step] for i in range(0, block.shape[1], step))


def row_sums(block):
    if block.shape[1] < LANES:
        return to_row(jnp.sum(block, axis=1, keepdims=True))
    return jnp.sum(jnp.transpose(block), axis=0, keepdims=True)


def kernel(
    ctx_size,
    head_size,
    answer_len,
    kv_here,
    bs_hbm,
    q_hbm,
    k_hbm,
    v_hbm,
    nk_hbm,
    nv_hbm,
    keep_hbm,
    w_hbm,
    readout_hbm,
    gain_hbm,
    proj_ref,
    summary_ref,
    solver_ref,
    bs_ref,
    q_ref,
    k_ref,
    v_ref,
    nk_ref,
    nv_ref,
    keep_ref,
    w_ref,
    readout_ref,
    gain_ref,
    mean_all,
    lse_all,
    flat_ref,
    y_ref,
    order_ref,
    left_ref,
    half_ref,
    give_ref,
    far_half,
    sum_ref,
    stat_all,
    local_sem,
    arrive_sem,
    sent_sem,
):
    grp = lax.axis_index("grp")
    mine = lax.axis_index("ctx")
    core = lax.axis_index("head")
    pairs, width = q_ref.shape
    heads = pairs // answer_len
    group = heads // kv_here
    tokens = k_ref.shape[0]
    sources, ablations = keep_ref.shape
    slots = slot_count(ctx_size, pairs)
    lines = flat_ref.shape[0] // pairs * answer_len
    compact = len(left_ref.shape) == 3
    sides, _, wide = w_ref.shape
    half = wide * sides // head_size
    chunk = half_ref.shape[3]
    partner = lax.rem(core + 1, head_size)
    turn = [partner, core]
    theirs, ours = (0, 1) if compact else (partner, core)
    scale = width ** (-0.5)
    rows = ablations * answer_len
    per = LANES // pairs
    devices = ctx_size * head_size

    def flips(position, size):
        return [bit * (1 - 2 * lax.rem(position // bit, 2)) for bit in powers(size)]

    ctx_flips, core_flips = flips(mine, ctx_size), flips(core, head_size)

    def flipped(position, deltas, mask):
        for i, delta in enumerate(deltas):
            if mask >> i & 1:
                position = position + delta
        return position

    def other(mask):
        return (
            grp,
            flipped(mine, ctx_flips, mask // head_size),
            flipped(core, core_flips, mask % head_size),
        )

    barrier = pltpu.get_barrier_semaphore()
    for mask in range(devices - 1, 0, -1):
        pl.semaphore_signal(
            barrier, inc=1, device_id=other(mask), device_id_type=pl.DeviceIdType.MESH
        )

    loads = [
        pltpu.make_async_copy(source, target, local_sem.at[min(max(i, 1), 3) - 1])
        for i, (source, target) in enumerate(
            (
                (q_hbm, q_ref),
                (k_hbm, k_ref),
                (v_hbm, v_ref),
                (nk_hbm, nk_ref),
                (nv_hbm, nv_ref),
                (keep_hbm, keep_ref),
                (bs_hbm, bs_ref),
                (readout_hbm, readout_ref),
                (gain_hbm, gain_ref),
            )
        )
    ]
    for copy in loads:
        copy.start()
    copies_w = [
        pltpu.make_async_copy(
            w_hbm.at[:, pl.ds(pl.multiple_of(turn[j] * half, LANES), half)] if compact else w_hbm,
            w_ref.at[j],
            local_sem.at[3],
        )
        for j in range(sides)
    ]
    for copy in copies_w:
        copy.start()

    loads[0].wait()
    loads[1].wait()
    queries = q_ref[...]
    scores = lax.dot_general(queries, k_ref[...], NT, preferred_element_type=F32) * scale
    near = lax.rem(iota((pairs, tokens), 1), kv_here) == lax.rem(
        iota((pairs, tokens), 0) // group, kv_here
    )
    top = jnp.max(jnp.where(near, scores, LOW), axis=1, keepdims=True)
    expo = jnp.where(near, jnp.exp(scores - top), 0.0)
    total = jnp.sum(expo, axis=1, keepdims=True)
    loads[2].wait()
    summed = jnp.dot(expo.astype(BF16), v_ref[...], preferred_element_type=F32)
    mean = summed / total
    lse = top + jnp.log(total)
    lse_all[mine] = to_row(jnp.concatenate([lse] * per, axis=0))
    pieces = mean_all.shape[0]
    some = heads // pieces
    for piece in range(pieces):
        for t in range(answer_len):
            first = t * heads + piece * some
            mean_all[piece, mine, pl.ds(t * some, some), :] = mean[first : first + some].astype(
                BF16
            )

    pl.semaphore_wait(barrier, devices - 1)

    sent_mean, sent_lse, sent_half, sent_stat = [sent_sem.at[i] for i in range(4)]
    parts = half // chunk
    arrive_mean = [arrive_sem.at[piece] for piece in range(pieces)]
    arrive_half = [arrive_sem.at[pieces + part] for part in range(parts)]
    arrive_stat = arrive_sem.at[pieces + parts]
    arrive_lse = arrive_sem.at[pieces + parts + 1]

    def remote(source, target, send, recv, device):
        return pltpu.make_async_remote_copy(
            src_ref=source,
            dst_ref=target,
            send_sem=send,
            recv_sem=recv,
            device_id=device,
            device_id_type=pl.DeviceIdType.MESH,
        )

    def to_peer(source, send, recv, k):
        place = ctx_size - 1 - k
        peer = jnp.where(place <= mine, place - 1, place)
        remote(source, source, send, recv, (grp, peer, core)).start()

    def bytes_of(block, send, recv):
        return remote(block, block, send, recv, (grp, mine, partner))

    all_lse = bytes_of(lse_all.at[pl.ds(0, ctx_size - 1)], sent_lse, arrive_lse)
    all_mean = [
        bytes_of(mean_all.at[piece, pl.ds(0, ctx_size - 1)], sent_mean, arrive_mean[piece])
        for piece in range(pieces)
    ]

    def send_to(peers, kinds):
        for kind in kinds:
            for k in peers:
                if kind < 0:
                    to_peer(lse_all.at[mine], sent_lse, arrive_lse, k)
                else:
                    to_peer(mean_all.at[kind, mine], sent_mean, arrive_mean[kind], k)

    first = range(1)
    later = range(1, ctx_size - 1)
    send_to(range(ctx_size - 1), [-1])
    send_to(first, range(pieces))
    send_to(later, range(pieces))

    for copy in loads[3:]:
        copy.wait()
    owns = nk_ref.shape[0]
    own_scores = lax.dot_general(queries, nk_ref[...], NT, preferred_element_type=F32) * scale
    place = iota((pairs, owns), 1)
    pair = iota((pairs, owns), 0)
    allowed = (lax.rem(place, kv_here) == lax.rem(pair // group, kv_here)) & (
        place // kv_here <= pair // heads
    )
    own_top = jnp.max(jnp.where(allowed, own_scores, LOW), axis=1, keepdims=True)
    own_expo = jnp.where(allowed, jnp.exp(own_scores - own_top), 0.0)
    own_total = jnp.sum(own_expo, axis=1, keepdims=True)
    own_probs = own_expo.astype(BF16).astype(F32)
    own_values = nv_ref[...].astype(F32)
    own_sum = jnp.zeros((pairs, width), F32)
    for i in range(owns):
        own_sum += own_probs[:, i : i + 1] * own_values[i : i + 1, :]
    flat_ref[pl.ds(ctx_size * pairs, pairs), :] = own_sum / own_total
    for slot in range(ctx_size + 1, flat_ref.shape[0] // pairs):
        flat_ref[pl.ds(slot * pairs, pairs), :] = jnp.zeros((pairs, width), F32)
    own_lse = to_row(jnp.concatenate([own_top + jnp.log(own_total)] * per, axis=0))

    keep = keep_ref[...].astype(F32)
    repeat = (iota((rows, ablations), 0) // answer_len == iota((rows, ablations), 1)).astype(F32)
    keep_rows = lax.dot_general(repeat, keep, NT, preferred_element_type=F32)
    lane = iota((1, LANES), 1)
    part = lane // pairs
    same = lax.rem(iota((rows, LANES), 1), pairs) // heads == lax.rem(
        iota((rows, LANES), 0), answer_len
    )
    masks = []
    for tile in range(slots // per):
        source = jnp.full((1, LANES), -1, jnp.int32)
        own_lane = jnp.zeros((1, LANES), F32)
        for k in range(per):
            slot = tile * per + k
            if slot < ctx_size:
                source = jnp.where(part == k, bs_ref[slot], source)
            if slot == ctx_size:
                own_lane = jnp.where(part == k, 1.0, own_lane)
        chosen = (iota((sources, LANES), 0) == source).astype(F32)
        kept = jnp.dot(keep_rows, chosen, preferred_element_type=F32) + own_lane
        masks.append((kept > 0.5) & same)

    eye = (iota((sources, sources), 0) == iota((sources, sources), 1)).astype(F32)
    keep_cols = lax.dot_general(keep, repeat, NT, preferred_element_type=F32)
    gram = lax.dot_general(keep, keep, NT, preferred_element_type=F32)
    count = jnp.sum(keep, axis=1, keepdims=True)
    count_row = jnp.sum(keep_rows, axis=0, keepdims=True) / answer_len
    system = gram - count * count_row / ablations + RIDGE * eye
    centered = keep_cols - count / ablations

    def sweep(k, state):
        on_row = iota((sources, sources), 0) == k
        on_col = iota((sources, sources), 1) == k
        row = jnp.sum(jnp.where(on_row, state, 0.0), axis=0, keepdims=True)
        col = jnp.sum(jnp.where(on_col, state, 0.0), axis=1, keepdims=True)
        pivot = jnp.sum(jnp.where(on_col[0:1], row, 0.0), axis=1, keepdims=True)
        inverse = 1.0 / pivot
        return jnp.where(
            on_row,
            jnp.where(on_col, -inverse, row * inverse),
            jnp.where(on_col, col * inverse, state - col * (row * inverse)),
        )

    swept = lax.fori_loop(0, sources, sweep, system, unroll=sources <= 8)
    solver_ref[...] = -jnp.dot(swept, centered, precision=lax.Precision.HIGHEST, preferred_element_type=F32)

    if compact:
        spot = iota((1, heads * lines), 1)
        line = lax.rem(spot, lines)
        wanted = (
            line // answer_len * pairs + lax.rem(line, answer_len) * heads + spot // lines
        )
        order_ref[...] = (iota(order_ref.shape, 0) == wanted).astype(BF16)
    all_lse.wait_recv()

    def make_coef():
        tops = []
        for tile in range(slots // per):
            line = jnp.full((1, LANES), LOW, F32)
            for k in range(per):
                slot = tile * per + k
                if slot <= ctx_size:
                    here = lse_all[slot] if slot < ctx_size else own_lse
                    line = jnp.where(part == k, here, line)
            tops.append(jnp.where(masks[tile], line, LOW))

        def across(value, op):
            shift = pairs
            while shift < LANES:
                value = op(value, pltpu.roll(value, shift, 1))
                shift *= 2
            return value

        overall = across(functools.reduce(jnp.maximum, tops), jnp.maximum)
        weights = [jnp.where(m, jnp.exp(s - overall), 0.0) for m, s in zip(masks, tops)]
        denom = across(functools.reduce(jnp.add, weights), jnp.add)
        inverse = 1.0 / jnp.where(same, denom, 1.0)
        coef = jnp.concatenate([(w * inverse).astype(BF16) for w in weights], axis=1)

        return coef

    def arrange(coef):
        if compact:
            coef = jnp.dot(coef, order_ref[...], preferred_element_type=F32).astype(BF16)
        return coef

    pair_up = 2

    def lines_of(k):
        return flat_ref[pl.ds(k, lines, stride=heads), :].astype(BF16)

    def project(j, h):
        outs = []
        for k in range(h, h + pair_up):
            left = (
                left_ref[h // pair_up, pl.ds((k - h) * lines, lines), :] if compact else lines_of(k)
            )
            outs.append(
                jnp.dot(
                    left, w_ref[j, pl.ds(k * width, width), :], preferred_element_type=F32
                )
            )
        if compact:
            y_ref[j, pl.ds(h * lines, pair_up * lines), :] = jnp.concatenate(
                outs, axis=0
            ).astype(BF16)
        else:
            for k in range(pair_up):
                for c in range(wide // LANES):
                    y_ref[c, pl.ds(h + k, lines, stride=heads), :] = outs[k][
                        :, c * LANES : (c + 1) * LANES
                    ]

    def mix(j, part):
        if compact:
            right = y_ref[j, :, pl.ds(part * chunk, chunk)]
        else:
            right = jnp.concatenate(
                [y_ref[c].astype(BF16) for c in range(wide // LANES)], axis=1
            )[:, j * half : (j + 1) * half]
        half_ref[j, part] = jnp.dot(coef, right, preferred_element_type=F32)

    for copy in copies_w:
        copy.wait()
    natural = make_coef()
    swaps = []
    for piece in range(pieces):
        all_mean[piece].wait_recv()
        for slot in range(ctx_size):
            for t in range(answer_len):
                flat_ref[pl.ds(slot * pairs + t * heads + piece * some, some), :] = mean_all[
                    piece, slot, pl.ds(t * some, some), :
                ].astype(F32)
        here = range(piece * some, (piece + 1) * some, pair_up)
        if piece == 0:
            coef = arrange(natural)
        for h in here:
            if compact:
                left_ref[h // pair_up] = jnp.concatenate(
                    [lines_of(k) for k in range(h, h + pair_up)], axis=0
                )
            project(0, h)
    for part in range(half // chunk):
        for j in range(1 if compact else head_size):
            mix(j, part)
        give_ref[part] = half_ref[theirs, part].astype(BF16)
        copy = remote(
            give_ref.at[part],
            far_half.at[part],
            sent_half,
            arrive_half[part],
            (grp, mine, partner),
        )
        copy.start()
        swaps.append(copy)
    if compact:
        for h in range(0, heads, pair_up):
            project(1, h)
        for part in range(half // chunk):
            mix(1, part)
    row_token = lax.rem(iota((rows, chunk), 0), answer_len)
    squared, read = 0.0, 0.0
    for part, copy in enumerate(swaps):
        here = pl.ds(part * chunk, chunk)
        reader = [
            readout_ref[t : t + 1, here].astype(F32) * gain_ref[:, here]
            for t in range(answer_len)
        ]
        reading = jnp.broadcast_to(reader[0], (rows, chunk))
        for t in range(1, answer_len):
            reading = jnp.where(row_token == t, reader[t], reading)
        copy.wait_recv()
        block = (half_ref[ours, part] + far_half[part].astype(F32)).astype(BF16)
        feature = block.astype(F32)
        sum_ref[part] = block
        squared += fold(feature * feature)
        read += fold(feature * reading)
    squares, dotted = row_sums(squared), row_sums(read)
    me = mine * head_size + core
    stat_all[me] = jnp.concatenate([squares, dotted], axis=0)
    for mask in range(devices - 1, 0, -1):
        remote(stat_all.at[me], stat_all.at[me], sent_stat, arrive_stat, other(mask)).start()
    all_stat = bytes_of(stat_all.at[pl.ds(0, devices - 1)], sent_stat, arrive_stat)
    all_lse.wait_send()
    for part in range(parts):
        proj_ref[:, :, pl.ds(part * chunk, chunk)] = (
            sum_ref[part].astype(F32).reshape(ablations, answer_len, chunk).astype(BF16)
        )
    all_stat.wait_recv()
    summary = stat_all[0]
    for i in range(1, devices):
        summary = summary + stat_all[i]
    summary_ref[...] = summary
    for copy in (
        bytes_of(mean_all.at[:, pl.ds(0, ctx_size - 1)], sent_mean, arrive_lse),
        bytes_of(far_half, sent_half, arrive_lse),
        all_stat,
    ):
        copy.wait_send()


def finish(
    answer_len,
    features,
    proj_ref,
    summary_ref,
    solver_ref,
    proj_out,
    logit_out,
    attr_out,
    logit_ref,
    attr_ref,
    sem,
):
    ablations = proj_ref.shape[0]
    sources = solver_ref.shape[0]
    rows = ablations * answer_len
    stores = [pltpu.make_async_copy(proj_ref, proj_out, sem.at[0])]
    stores[0].start()
    summary, solver = summary_ref[...], solver_ref[...]
    logits = summary[1:2] * lax.rsqrt(summary[0:1] / features + EPSILON)
    spread = jnp.transpose(jnp.broadcast_to(logits, (LANES, LANES)))
    picked = jnp.where(
        iota((rows, ablations), 0) // answer_len == iota((rows, ablations), 1),
        spread[:, :ablations],
        0.0,
    )
    row_of = lax.rem(iota((rows, ablations), 0), answer_len)
    for t in range(answer_len):
        logit_ref[t : t + 1, :] = jnp.sum(
            jnp.where(row_of == t, picked, 0.0), axis=0, keepdims=True
        )
    target_dev = logits - jnp.sum(logits, axis=1, keepdims=True) / rows
    answer = jnp.sum(solver * target_dev, axis=1, keepdims=True)
    diagonal = iota((sources, sources), 0) == iota((sources, sources), 1)
    attr_ref[...] = jnp.sum(jnp.where(diagonal, answer, 0.0), axis=0, keepdims=True)
    stores.append(pltpu.make_async_copy(logit_ref, logit_out, sem.at[0]))
    stores.append(pltpu.make_async_copy(attr_ref, attr_out, sem.at[0]))
    for copy in stores[1:]:
        copy.start()
    for copy in stores:
        copy.wait()


def on_device(
    ctx_size,
    head_size,
    queries,
    keys,
    values,
    new_keys,
    new_values,
    keep,
    block_source,
    out_weight,
    readout,
    gain,
):
    answer_len, heads, width = queries.shape
    tokens, kv_here, _ = keys.shape
    assert tokens == BLOCK
    pairs = answer_len * heads
    ablations, sources = keep.shape
    rows = ablations * answer_len
    depth, columns = out_weight.shape
    half = columns // head_size
    per = LANES // pairs
    assert rows == LANES and per * pairs == LANES and width == LANES
    slots = slot_count(ctx_size, pairs)
    lines = -(-slots * answer_len // 8) * 8
    compact = lines <= 32 and half % LANES == 0
    if not compact:
        lines = slots * answer_len
    devices = ctx_size * head_size
    pieces = 2
    sides = head_size if compact else 1
    chunk = half
    parts = half // chunk
    assert head_size == 2
    assert all(size & (size - 1) == 0 for size in (ctx_size, head_size))
    hbm = pl.BlockSpec(memory_space=pltpu.HBM)
    vmem = pl.BlockSpec(memory_space=pltpu.VMEM)
    projected, summary, solver = pl.pallas_call(
        functools.partial(kernel, ctx_size, head_size, answer_len, kv_here),
        out_shape=(
            jax.ShapeDtypeStruct((ablations, answer_len, half), BF16),
            jax.ShapeDtypeStruct((2, rows), F32),
            jax.ShapeDtypeStruct((sources, rows), F32),
        ),
        in_specs=[hbm] * 10,
        out_specs=(vmem, vmem, vmem),
        scratch_shapes=[
            pltpu.SMEM((ctx_size,), jnp.int32),
            pltpu.VMEM((pairs, width), BF16),
            pltpu.VMEM((tokens * kv_here, width), BF16),
            pltpu.VMEM((tokens * kv_here, width), BF16),
            pltpu.VMEM((answer_len * kv_here, width), BF16),
            pltpu.VMEM((answer_len * kv_here, width), BF16),
            pltpu.VMEM((sources, ablations), jnp.int32),
            pltpu.VMEM((sides, depth, columns // sides), BF16),
            pltpu.VMEM((answer_len, half), BF16),
            pltpu.VMEM((1, half), F32),
            pltpu.VMEM((pieces, ctx_size, pairs // pieces, width), BF16),
            pltpu.VMEM((ctx_size, 1, LANES), F32),
            pltpu.VMEM((heads * lines, width), F32),
            pltpu.VMEM((head_size, heads * lines, half), BF16)
            if compact
            else pltpu.VMEM((columns // LANES, heads * lines, LANES), F32),
            pltpu.VMEM((slots * pairs, heads * lines) if compact else (8, LANES), BF16),
            pltpu.VMEM((heads // 2, 2 * lines, width) if compact else (16, LANES), BF16),
            pltpu.VMEM((head_size, parts, rows, chunk), F32),
            pltpu.VMEM((parts, rows, chunk), BF16),
            pltpu.VMEM((parts, rows, chunk), BF16),
            pltpu.VMEM((parts, rows, chunk), BF16),
            pltpu.VMEM((devices, 2, LANES), F32),
            pltpu.SemaphoreType.DMA((4,)),
            pltpu.SemaphoreType.DMA((pieces + parts + 2,)),
            pltpu.SemaphoreType.DMA((4,)),
        ],
        compiler_params=pltpu.CompilerParams(
            collective_id=0, has_side_effects=True, vmem_limit_bytes=48 << 20
        ),
        name="attribute",
    )(
        *(pltpu.with_memory_space_constraint(x, pltpu.HBM) for x in (
        block_source,
        queries.reshape(pairs, width),
        keys.reshape(tokens * kv_here, width),
        values.reshape(tokens * kv_here, width),
        new_keys.reshape(-1, width),
        new_values.reshape(-1, width),
        keep.T,
        out_weight,
        readout,
        gain.reshape(1, -1),
        )),
    )
    projected, logits, attribution = pl.pallas_call(
        functools.partial(finish, answer_len, columns * ctx_size),
        out_shape=(
            jax.ShapeDtypeStruct(projected.shape, BF16),
            jax.ShapeDtypeStruct((answer_len, ablations), F32),
            jax.ShapeDtypeStruct((1, sources), F32),
        ),
        in_specs=[vmem] * 3,
        compiler_params=pltpu.CompilerParams(vmem_limit_bytes=2 << 20),
        out_specs=[hbm] * 3,
        scratch_shapes=[
            pltpu.VMEM((answer_len, ablations), F32),
            pltpu.VMEM((1, sources), F32),
            pltpu.SemaphoreType.DMA((1,)),
        ],
        name="finish",
    )(projected, summary, solver)
    return projected, logits.T, attribution.reshape(sources)


def solution(mesh):
    in_specs = (
        P("grp", "head", None),
        P(("grp", "ctx"), "head", None),
        P(("grp", "ctx"), "head", None),
        P("grp", "head", None),
        P("grp", "head", None),
        P("grp", None),
        P("grp"),
        P("head", "ctx"),
        P("grp", ("ctx", "head")),
        P(("ctx", "head")),
    )
    out_specs = (P("grp", None, ("ctx", "head")), P("grp", None), P("grp"))
    return jax.shard_map(
        functools.partial(on_device, mesh.shape["ctx"], mesh.shape["head"]),
        mesh=mesh,
        in_specs=in_specs,
        out_specs=out_specs,
        check_vma=False,
    )
```
